512 devices in a mesh: grp: 16 (over y, x), tile: 32 (over z, core).
Axes of the slice: x: 4, y: 4, z: 16, core: 2. Of those that a mesh axis runs over, the one named last changes fastest.
Arguments:
- jac_point: float32 [6, 2097152], P(None, ('grp', 'tile')), may hold values from -6 to 6
- jac_cam: float32 [18, 2097152], P(None, ('grp', 'tile')), may hold values from -3 to 3
- resid: float32 [2, 2097152], P(None, ('grp', 'tile')), may hold values from -6 to 6
- point_index: int32 [2097152], P(('grp', 'tile')), may hold values from 0 to 4095, as said below
- cam_index: int32 [2097152], P(('grp', 'tile')), may hold values from 0 to 12287, as said below
Outputs:
- point_step: float32 [3, 2097152], P(None, ('grp', 'tile'))
- camera_step: float32 [9, 196608], P(None, ('grp', 'tile'))
- point_resid: float32 [3, 2097152], P(None, ('grp', 'tile'))
- camera_resid: float32 [9, 196608], P(None, ('grp', 'tile'))
The draws below stay inside these ranges and needn't reach their ends.
Inputs may be any that keep to these rules, and one draw needn't show every extreme that they name: `point_index`: index among the points of the observation's own device; every device names point 0 and point 4096 - 1. `cam_index`: block h of a device's observations (slots h * 256 to (h + 1) * 256 - 1) names cameras of group h by their index within the group; every block names camera 0 and camera 12288 - 1.
All inputs are finite; a program needn't handle non-finite values.
Results may differ from the reference program's by a relative error of at most 0.0002.
Values sent between devices are 32-bit elements; how exact they have to be, the bound alone decides.
A program may use at most 64 MiB of HBM per device.

```python
import jax
import jax.numpy as jnp
from jax import lax

SLOT = 256
P_DEV = 4096
ITERS = 2
OBS_DEV = 4096
CAM_GRP = 12288
CAMS = 196608
OBS = 2097152
N_GRP = 16
N_TILE = 32


def draw_point_index(key, part):
    values = jax.random.randint(key, (OBS,), 0, P_DEV, dtype=jnp.int32)
    blocks = values.reshape(-1, OBS_DEV)
    blocks = blocks.at[:, 0].set(0).at[:, 1].set(P_DEV - 1)
    return blocks.reshape(OBS)


def draw_cam_index(key, part):
    keys = jax.random.split(jax.random.fold_in(key, 7), 5)
    lowest = jax.random.randint(keys[0], (OBS,), 0, CAM_GRP, dtype=jnp.int32)
    for number in range(1, 4):
        lowest = jnp.minimum(lowest, jax.random.randint(keys[number], (OBS,), 0, CAM_GRP, dtype=jnp.int32))
    shuffle = jax.random.permutation(keys[4], CAM_GRP).astype(jnp.int32)
    values = shuffle[lowest]
    blocks = values.reshape(-1, SLOT)
    blocks = blocks.at[:, 0].set(0).at[:, 1].set(CAM_GRP - 1)
    return blocks.reshape(OBS)


def steps_of(key, shape, shards, low, top_value):
    loudness, own = 1.0, jax.random.fold_in(key, 6)
    for position, parts in shards:
        draws = jnp.exp(jax.random.uniform(jax.random.fold_in(own, position), (parts,), jnp.float32, low / len(shards), top_value / len(shards)))
        loudness = loudness * jnp.repeat(draws, shape[position] // parts).reshape([-1 if axis == position else 1 for axis in range(len(shape))])
    return loudness


def scatter_about(key, dims, width, bound, cuts=(), kind=jnp.bfloat16):
    values = jax.random.normal(key, dims, jnp.float32) * width
    if len(cuts) > 0:
        values = steps_of(key, dims, cuts, -0.22, 0.18) * values
    return jnp.clip(values, min=-bound, max=bound).astype(kind)


def setup_inputs(seed: int = 0) -> dict:
    key_list = jax.random.split(jax.random.key(seed), 6)
    jac_point = scatter_about(key_list[0], (6, OBS), 1.0, 6.0, ((1, 512),), jnp.float32)
    jac_cam = scatter_about(key_list[1], (18, OBS), 0.5, 3.0, ((1, 512),), jnp.float32)
    resid = scatter_about(key_list[2], (2, OBS), 1.0, 6.0, ((1, 512),), jnp.float32)
    point_index = draw_point_index(jax.random.fold_in(key_list[5], 71), 0)
    cam_index = draw_cam_index(jax.random.fold_in(key_list[5], 71), 0)
    return dict(jac_point=jac_point, jac_cam=jac_cam, resid=resid, point_index=point_index, cam_index=cam_index)


damping = 1.0


def segment_rows(data, ids, count):
    return jax.vmap(lambda row: jax.ops.segment_sum(row, ids, num_segments=count))(data)


def reference(jac_point, jac_cam, resid, point_index, cam_index):
    devices = N_GRP * N_TILE
    block_of = jnp.arange(OBS_DEV, dtype=jnp.int32) // SLOT
    device_ids = jnp.arange(devices, dtype=jnp.int32)

    def local(dev):
        start = dev * OBS_DEV
        jp = lax.dynamic_slice_in_dim(jac_point, start, OBS_DEV, 1).reshape(2, 3, OBS_DEV)
        jc = lax.dynamic_slice_in_dim(jac_cam, start, OBS_DEV, 1).reshape(2, 9, OBS_DEV)
        res = lax.dynamic_slice_in_dim(resid, start, OBS_DEV, 1)
        pts = lax.dynamic_slice_in_dim(point_index, start, OBS_DEV, 0)
        cams = block_of * CAM_GRP + lax.dynamic_slice_in_dim(cam_index, start, OBS_DEV, 0)
        return jp, jc, res, pts, cams

    def spread(stacked, rows):
        return jnp.transpose(stacked, (1, 0, 2)).reshape(rows, devices * P_DEV)

    def init_step(acc, dev):
        jp, jc, res, pts, cams = local(dev)
        point_terms = jnp.concatenate([-jnp.sum(jp * res[:, None], axis=0), jnp.sum(jp * jp, axis=0)], axis=0)
        cam_terms = jnp.concatenate([-jnp.sum(jc * res[:, None], axis=0), jnp.sum(jc * jc, axis=0)], axis=0)
        return acc + segment_rows(cam_terms, cams, CAMS), segment_rows(point_terms, pts, P_DEV)

    cam_init, point_init = lax.scan(init_step, jnp.zeros((18, CAMS), jnp.float32), device_ids)
    point_init = spread(point_init, 6)

    def apply(vp, vc):
        def step(acc, dev):
            jp, jc, res, pts, cams = local(dev)
            own = lax.dynamic_slice_in_dim(vp, dev * P_DEV, P_DEV, 1)
            error = jnp.sum(jp * own[:, pts][None], axis=1) + jnp.sum(jc * vc[:, cams][None], axis=1)
            acc = acc + segment_rows(jnp.sum(jc * error[:, None], axis=0), cams, CAMS)
            return acc, segment_rows(jnp.sum(jp * error[:, None], axis=0), pts, P_DEV)

        cam_out, point_out = lax.scan(step, jnp.zeros((9, CAMS), jnp.float32), device_ids)
        return spread(point_out, 3) + damping * vp, cam_out + damping * vc

    point_rhs, point_diag = point_init[:3], point_init[3:]
    camera_rhs, camera_diag = cam_init[:9], cam_init[9:]
    point_pre = point_diag + damping
    camera_pre = camera_diag + damping
    point_x = jnp.zeros_like(point_rhs)
    camera_x = jnp.zeros_like(camera_rhs)
    point_r, camera_r = point_rhs, camera_rhs
    point_z, camera_z = point_r / point_pre, camera_r / camera_pre
    point_dir, camera_dir = point_z, camera_z
    norm_now = jnp.sum(point_r * point_z) + jnp.sum(camera_r * camera_z)
    for step_number in range(ITERS):
        point_q, camera_q = apply(point_dir, camera_dir)
        alpha = norm_now / (jnp.sum(point_dir * point_q) + jnp.sum(camera_dir * camera_q))
        point_x = point_x + alpha * point_dir
        camera_x = camera_x + alpha * camera_dir
        point_r = point_r - alpha * point_q
        camera_r = camera_r - alpha * camera_q
        if step_number + 1 < ITERS:
            point_z, camera_z = point_r / point_pre, camera_r / camera_pre
            norm_next = jnp.sum(point_r * point_z) + jnp.sum(camera_r * camera_z)
            ratio = norm_next / norm_now
            point_dir = point_z + ratio * point_dir
            camera_dir = camera_z + ratio * camera_dir
            norm_now = norm_next
    return point_x, camera_x, point_r, camera_r
```

```python
import functools

import jax
import jax.numpy as jnp
from jax import lax
from jax.experimental import pallas as pl
from jax.experimental.pallas import tpu as pltpu
from jax.sharding import PartitionSpec as P

F32, BF16, I32 = jnp.float32, jnp.bfloat16, jnp.int32
MESH = pl.DeviceIdType.MESH
SLOT = 256
CAM_DEV = 384
damping = 1.0


def spread(n, d):
    half = lax.div(d + 1, jnp.int32(2))
    return half * (2 * lax.rem(d, jnp.int32(2)) - 1) + n


def kernel(
    NG, OBS, NPTS,
    jp, jc, res, pidx, cidx,
    xp, xc, rp, rc,
    S, R2, OHC, OHP, LHS, LHSP, ACC, AROW, APROW, TV, TP,
    SB0, RB0, SB, RB, VB, CV, PV, PVEC,
    PTS, PTR, XS, XR, ER, EB, G, GZ, GP, XF, XG,
    loc, a2a_s, a2a_r, fwd_s, fwd_r, rs_s, rs_r, ag_s, ag_r,
    pt_s, pt_r, x_s, x_r, e_s, e_r, gz_s, gz_r, gp_s, gp_r, gq_s, gq_r, pm_s, pm_r,
):
    T = NG // 2
    ROWS = T * 32
    NA = NPTS // 256
    one = jnp.int32(1)
    ng = jnp.int32(NG)
    g = lax.axis_index("grp")
    tt = lax.axis_index("tile")
    z = lax.div(tt, jnp.int32(2))
    c = lax.rem(tt, jnp.int32(2))
    partner = (g, 2 * z + 1 - c)

    def z_at(k):
        d = lax.rem(ng - k, ng)
        return lax.rem(z + spread(ng, d), ng)

    def g_at(d):
        return lax.rem(g + d, ng)

    bar = pltpu.get_barrier_semaphore()

    @pl.loop(1, NG)
    def _(d):
        pl.semaphore_signal(bar, inc=1, device_id=(g, 2 * z_at(d) + c), device_id_type=MESH)
        pl.semaphore_signal(bar, inc=1, device_id=(g_at(d), tt), device_id_type=MESH)

    pl.semaphore_signal(bar, inc=1, device_id=partner, device_id_type=MESH)

    @pl.when(g != z)
    def _():
        pl.semaphore_signal(bar, inc=1, device_id=(z, 2 * g + c), device_id_type=MESH)

    @pl.loop(0, NG)
    def _(h):
        cols = pl.ds(pl.multiple_of(h * SLOT, SLOT), SLOT)
        S[h, 0:8, :] = jc[0:8, cols]
        S[h, 8:16, :] = jc[9:17, cols]
        S[h, 16:17, :] = jc[8:9, cols]
        S[h, 17:18, :] = jc[17:18, cols]
        S[h, 18:20, :] = res[:, cols]
        S[h, 20:21, :] = cidx[:, cols].astype(F32)

    G[...] = jnp.zeros_like(G)

    pl.semaphore_wait(bar, 2 * (NG - 1) + 1 + jnp.where(g != z, 1, 0))

    def a2a_copy(zt, zf):
        return pltpu.make_async_remote_copy(
            S.at[zt], R2.at[c, zf], a2a_s.at[zt], a2a_r.at[zf],
            device_id=(g, 2 * zt + c), device_id_type=MESH)

    own = pltpu.make_async_copy(S.at[z], R2.at[c, z], loc)
    own.start()

    @pl.loop(1, NG)
    def _(k):
        a2a_copy(z_at(k), z).start()

    def fold(v):
        out = v[:, 0:128]
        for i in range(1, v.shape[1] // 128):
            out = out + v[:, i * 128:(i + 1) * 128]
        return jnp.sum(out, axis=0, keepdims=True)

    def point_lhs(row0, cols, v, ap):
        v2 = jnp.concatenate([v, v], axis=0)
        low = lax.broadcasted_iota(I32, (16, SLOT), 0) < 8
        am = jnp.broadcast_to(ap, (16, SLOT)) - jnp.where(low, 0.0, 1.0)
        for i in range(NA // 2):
            LHSP[row0 + i * 16:row0 + i * 16 + 16, cols] = jnp.where(
                am == float(2 * i), v2, 0.0).astype(BF16)

    def split(v):
        hi = v.astype(BF16).astype(F32)
        return hi, v - hi

    nt = (((1,), (1,)), ((), ()))

    def point_sum(row0):
        out = lax.dot_general(LHSP[row0:row0 + NA * 8, :], OHP[...], nt,
                              preferred_element_type=F32)
        for a in range(NA):
            PV[:, a * 256:(a + 1) * 256] = out[a * 8:(a + 1) * 8, :]

    def point_gather(src, it):
        for i in range(NA // 2):
            parts = []
            for a in (2 * i, 2 * i + 1):
                hi, lo = split(PVEC[src, :, a * 256:(a + 1) * 256])
                parts += [hi, lo, jnp.zeros((2, 256), F32)]
            TP[i * 16:i * 16 + 16, :] = jnp.concatenate(parts, axis=0).astype(BF16)

        @pl.loop(0, NG)
        def _(k):
            h = z_at(k)
            cols = pl.ds(pl.multiple_of(h * SLOT, SLOT), SLOT)
            got = jnp.dot(TP[...], OHP[:, cols], preferred_element_type=F32)
            ap = jnp.broadcast_to(APROW[:, cols], (8, SLOT))
            acc = jnp.zeros((8, SLOT), F32)
            for a in range(NA):
                acc = jnp.where(ap == float(a), got[a * 8:(a + 1) * 8, :], acc)
            v = acc[0:3] + acc[3:6]
            PTS[it, h, :, 0:SLOT] = jnp.sum(jp[0:3, cols] * v, axis=0, keepdims=True)
            PTS[it, h, :, SLOT:2 * SLOT] = jnp.sum(jp[3:6, cols] * v, axis=0, keepdims=True)

            @pl.when(h != z)
            def _():
                pt_copy(it, h, z).start()

            @pl.when(h == z)
            def _():
                pltpu.make_async_copy(PTS.at[it, h], PTR.at[it, z], pt_r.at[it, z]).start()

    def pt_copy(it, zt, zf):
        return pltpu.make_async_remote_copy(
            PTS.at[it, zt], PTR.at[it, zf], pt_s.at[it, zt], pt_r.at[it, zf],
            device_id=(g, 2 * zt + c), device_id_type=MESH)

    @pl.loop(0, NG)
    def _(h):
        cols = pl.ds(pl.multiple_of(h * SLOT, SLOT), SLOT)
        p = pidx[:, cols]
        ap = lax.shift_right_logical(p, 8).astype(F32)
        n = (p & 255).astype(F32)
        APROW[:, cols] = ap
        row = lax.broadcasted_iota(I32, (256, SLOT), 0).astype(F32)
        OHP[:, cols] = jnp.where(row == jnp.broadcast_to(n, (256, SLOT)), 1.0, 0.0).astype(BF16)
        j0, j1 = jp[0:3, cols], jp[3:6, cols]
        s0, s1 = res[0:1, cols], res[1:2, cols]
        v = jnp.concatenate(
            [-(j0 * s0 + j1 * s1), j0 * j0 + j1 * j1, jnp.zeros((2, SLOT), F32)], axis=0)
        hi, lo = split(v)
        point_lhs(0, cols, hi, ap)
        point_lhs(NA * 8, cols, lo, ap)

    out = lax.dot_general(LHSP[...], OHP[...], nt, preferred_element_type=F32)
    for a in range(NA):
        PV[:, a * 256:(a + 1) * 256] = (
            out[a * 8:(a + 1) * 8, :] + out[(NA + a) * 8:(NA + a + 1) * 8, :])
    prhs = PV[0:3, :]
    pmat = PV[3:6, :] + damping
    pz = prhs / pmat
    PVEC[0] = prhs
    PVEC[1] = pmat
    PVEC[2] = pz
    G[0:1, :] += fold(prhs * pz)
    G[1:2, :] += fold(pz * pz)
    point_gather(2, 0)

    pat_row = lax.broadcasted_iota(I32, (32, SLOT), 0)
    pat = jnp.where(pat_row < 8, 0, jnp.where(
        pat_row < 16, 1, jnp.where(
            pat_row < 24, 2, jnp.where(pat_row < 27, pat_row - 24, 2000)))).astype(F32)

    def cam_lhs(row0, col0, v8, v1, am):
        h8, l8 = split(v8)
        h1, l1 = split(v1)
        h1 = jnp.broadcast_to(h1, (8, SLOT))
        l1 = jnp.broadcast_to(l1, (8, SLOT))
        hi = jnp.concatenate([h8, h8, h8, h1], axis=0)
        lo = jnp.concatenate([l8, l8, l8, l1], axis=0)
        for t in range(T):
            hit = am == float(3 * t)
            LHS[row0 + t * 32:row0 + t * 32 + 32, col0:col0 + SLOT] = (
                jnp.where(hit, hi, 0.0).astype(BF16))
            LHS[row0 + ROWS + t * 32:row0 + ROWS + t * 32 + 32, col0:col0 + SLOT] = (
                jnp.where(hit, lo, 0.0).astype(BF16))

    def jac(core, zs):
        return (R2[core, zs, 0:8, :], R2[core, zs, 8:16, :],
                R2[core, zs, 16:17, :], R2[core, zs, 17:18, :])

    def block(zs):
        return pl.ds(pl.multiple_of(zs * (2 * SLOT), 2 * SLOT), 2 * SLOT)

    def half_block(zs, core):
        return pl.ds(pl.multiple_of(zs * (2 * SLOT) + core * SLOT, SLOT), SLOT)

    def fwd_copy(core, zs):
        return pltpu.make_async_remote_copy(
            R2.at[core, zs], R2.at[core, zs], fwd_s.at[zs], fwd_r.at[zs],
            device_id=partner, device_id_type=MESH)

    ACC[...] = jnp.zeros_like(ACC)
    own.wait()
    fwd_copy(c, z).start()
    log_t = T.bit_length() - 1

    @pl.loop(0, NG)
    def _(k):
        @pl.when(k + 1 < NG)
        def _():
            zn = z_at(k + 1)
            a2a_copy(zn, zn).wait_recv()
            fwd_copy(c, zn).start()

        zs = z_at(k)
        fwd_copy(1 - c, zs).wait_recv()
        for core in range(2):
            idx = R2[core, zs, 20:21, :].astype(I32)
            q = lax.shift_right_logical(idx, 7)
            t = lax.shift_right_logical(q * 171, 9)
            tau = lax.shift_right_logical(t, 1)
            a = 3 * (tau & (T - 1)) + (q - 3 * t)
            a = jnp.where((t & 1) == c, a, -1000).astype(F32)
            n = (lax.shift_right_logical(tau, log_t) * 128 + (idx & 127)).astype(F32)
            AROW[:, half_block(zs, core)] = a
            row = lax.broadcasted_iota(I32, (256, SLOT), 0).astype(F32)
            OHC[:, half_block(zs, core)] = jnp.where(
                row == jnp.broadcast_to(n, (256, SLOT)), 1.0, 0.0).astype(BF16)
            am = jnp.broadcast_to(a, (32, SLOT)) - pat
            J0, J1, j0, j1 = jac(core, zs)
            s0, s1 = R2[core, zs, 18:19, :], R2[core, zs, 19:20, :]
            cam_lhs(0, core * SLOT, -(J0 * s0 + J1 * s1), -(j0 * s0 + j1 * s1), am)
            cam_lhs(2 * ROWS, core * SLOT, J0 * J0 + J1 * J1, j0 * j0 + j1 * j1, am)
        ACC[...] += lax.dot_general(LHS[...], OHC[:, block(zs)], nt, preferred_element_type=F32)

    def rs_copy(it, gt, gf):
        if it == 2:
            src, dst = SB0.at[gt], RB0.at[gf]
        else:
            src, dst = SB.at[it, gt], RB.at[it, gf]
        return pltpu.make_async_remote_copy(
            src, dst, rs_s.at[it, gt], rs_r.at[it, gf],
            device_id=(gt, tt), device_id_type=MESH)

    def rs_start(it):
        @pl.loop(1, NG)
        def _(d):
            rs_copy(it, g_at(d), g).start()

    for half in range(2):
        lanes = slice(half * 128, half * 128 + 128)
        for t in range(T):
            for part in range(2):
                r = 2 * ROWS * part + t * 32
                SB0[half * T + t, part * 32:part * 32 + 32, :] = (
                    ACC[r:r + 32, lanes] + ACC[r + ROWS:r + ROWS + 32, lanes])
    rs_start(2)

    def rs_sum(it, total):
        def step(d, total):
            gf = g_at(d)
            rs_copy(it, gf, gf).wait_recv()
            return total + (RB0[gf] if it == 2 else RB[it, gf])
        return lax.fori_loop(1, NG, step, total)

    both = rs_sum(2, SB0[g])
    crhs = both[0:32]
    cmat = both[32:64] + damping
    cz = crhs / cmat
    CV[0] = crhs
    CV[1] = cmat
    CV[2] = cz
    G[0:1, :] += fold(crhs * cz)
    G[1:2, :] += fold(cz * cz)

    def ag_copy(it, gt, gf):
        return pltpu.make_async_remote_copy(
            VB.at[it, gf], VB.at[it, gf], ag_s.at[it, gt], ag_r.at[it, gf],
            device_id=(gt, tt), device_id_type=MESH)

    def gather_all(it, v):
        VB[it, g] = v

        @pl.loop(1, NG)
        def _(d):
            ag_copy(it, g_at(d), g).start()

        @pl.loop(1, NG)
        def _(d):
            ag_copy(it, g_at(d), g_at(d)).wait_recv()

        for half in range(2):
            lanes = slice(half * 128, half * 128 + 128)
            for t in range(T):
                hi, lo = split(VB[it, half * T + t])
                TV[t * 32:t * 32 + 32, lanes] = hi.astype(BF16)
                TV[ROWS + t * 32:ROWS + t * 32 + 32, lanes] = lo.astype(BF16)

    def x_copy(it, zs):
        pair = pl.ds(2 * zs, 2)
        return pltpu.make_async_remote_copy(
            XS.at[it, pair], XR.at[it, pair], x_s.at[it, zs], x_r.at[it, zs],
            device_id=partner, device_id_type=MESH)

    def cam_terms(it):
        @pl.loop(0, NG)
        def _(k):
            zs = z_at(k)
            got = jnp.dot(TV[...], OHC[:, block(zs)], preferred_element_type=F32)
            pltpu.make_async_copy(PTR.at[it, zs], PTR.at[it, zs], pt_r.at[it, zs]).wait()
            for core in range(2):
                cols = slice(core * SLOT, core * SLOT + SLOT)
                am = jnp.broadcast_to(AROW[:, half_block(zs, core)], (32, SLOT)) - pat
                acc = jnp.zeros((32, SLOT), F32)
                for t in range(T):
                    acc = jnp.where(
                        am == float(3 * t),
                        got[t * 32:t * 32 + 32, cols]
                        + got[ROWS + t * 32:ROWS + t * 32 + 32, cols], acc)
                v8 = acc[0:8] + acc[8:16] + acc[16:24]
                v1 = jnp.sum(acc[24:32], axis=0, keepdims=True)
                J0, J1, j0, j1 = jac(core, zs)
                mine = jnp.where(c == core, 1.0, 0.0)
                XS[it, 2 * zs + core, :, 0:SLOT] = (
                    jnp.sum(J0 * v8, axis=0, keepdims=True) + j0 * v1
                    + mine * PTR[it, zs, :, 0:SLOT])
                XS[it, 2 * zs + core, :, SLOT:2 * SLOT] = (
                    jnp.sum(J1 * v8, axis=0, keepdims=True) + j1 * v1
                    + mine * PTR[it, zs, :, SLOT:2 * SLOT])
            x_copy(it, zs).start()

    def e_copy(it, zt, zf):
        return pltpu.make_async_remote_copy(
            ER.at[it, 2 * zt + c], EB.at[it, zf], e_s.at[it, zt], e_r.at[it, zf],
            device_id=(g, 2 * zt + c), device_id_type=MESH)

    def cam_scatter(it):
        ACC[0:2 * ROWS, :] = jnp.zeros((2 * ROWS, 256), F32)

        @pl.loop(0, NG)
        def _(k):
            zs = z_at(k)
            x_copy(it, zs).wait_recv()
            for core in range(2):
                e = XS[it, 2 * zs + core] + XR[it, 2 * zs + core]
                ER[it, 2 * zs + core] = e
                e0, e1 = e[:, 0:SLOT], e[:, SLOT:2 * SLOT]
                J0, J1, j0, j1 = jac(core, zs)
                am = jnp.broadcast_to(AROW[:, half_block(zs, core)], (32, SLOT)) - pat
                cam_lhs(0, core * SLOT, J0 * e0 + J1 * e1, j0 * e0 + j1 * e1, am)

            @pl.when(zs != z)
            def _():
                e_copy(it, zs, z).start()

            @pl.when(zs == z)
            def _():
                pltpu.make_async_copy(ER.at[it, 2 * zs + c], EB.at[it, z], e_r.at[it, z]).start()

            mine = ER[it, 2 * zs + c]
            if it == 0:
                G[2:3, :] += fold(mine * mine)
            else:
                before = ER[0, 2 * zs + c]
                G[6:7, :] += fold(mine * before)
                G[7:8, :] += fold(mine * mine)
            ACC[0:2 * ROWS, :] += lax.dot_general(
                LHS[0:2 * ROWS, :], OHC[:, block(zs)], nt, preferred_element_type=F32)

        for half in range(2):
            lanes = slice(half * 128, half * 128 + 128)
            for t in range(T):
                SB[it, half * T + t] = (
                    ACC[t * 32:t * 32 + 32, lanes]
                    + ACC[ROWS + t * 32:ROWS + t * 32 + 32, lanes])
        rs_start(it)

    def point_scatter(it):
        @pl.loop(0, NG)
        def _(k):
            h = z_at(k)
            cols = pl.ds(pl.multiple_of(h * SLOT, SLOT), SLOT)
            pltpu.make_async_copy(EB.at[it, h], EB.at[it, h], e_r.at[it, h]).wait()
            e0, e1 = EB[it, h, :, 0:SLOT], EB[it, h, :, SLOT:2 * SLOT]
            hi, lo = split(jp[0:3, cols] * e0 + jp[3:6, cols] * e1)
            v = jnp.concatenate([hi, lo, jnp.zeros((2, SLOT), F32)], axis=0)
            point_lhs(0, cols, v, APROW[:, cols])

        point_sum(0)
        return PV[0:3, :] + PV[3:6, :]

    gather_all(0, cz)
    cam_terms(0)
    cam_scatter(0)
    pq = point_scatter(0) + damping * PVEC[2]
    pw = pq / PVEC[1]
    PVEC[3] = pq
    PVEC[4] = pw
    point_gather(4, 1)
    G[3:4, :] += fold(pq * pw)
    G[4:5, :] += fold(PVEC[2] * pw)
    G[5:6, :] += fold(pw * pw)

    cq = rs_sum(0, SB[0, g]) + damping * CV[2]
    cw = cq / CV[1]
    CV[3] = cq
    CV[4] = cw
    G[3:4, :] += fold(cq * cw)
    G[4:5, :] += fold(CV[2] * cw)
    G[5:6, :] += fold(cw * cw)
    gather_all(1, cw)
    cam_terms(1)
    cam_scatter(1)

    def gz_copy(zt, zf):
        return pltpu.make_async_remote_copy(
            G, GZ.at[zf], gz_s.at[zt], gz_r.at[zf],
            device_id=(g, 2 * zt + c), device_id_type=MESH)

    def gp_copy(gt, gf):
        return pltpu.make_async_remote_copy(
            GP.at[gf], GP.at[gf], gp_s.at[gt], gp_r.at[gf],
            device_id=(gt, tt), device_id_type=MESH)

    @pl.loop(1, NG)
    def _(k):
        gz_copy(z_at(k), z).start()

    def gz_step(k, total):
        zs = z_at(k)
        gz_copy(zs, zs).wait_recv()
        return total + GZ[zs]

    gsum = lax.fori_loop(1, NG, gz_step, G[...])
    GP[g] = gsum

    @pl.loop(1, NG)
    def _(d):
        gp_copy(g_at(d), g).start()

    PVEC[5] = point_scatter(1) + damping * PVEC[4]

    def gp_step(d, total):
        gf = g_at(d)
        gp_copy(gf, gf).wait_recv()
        return total + GP[gf]

    GZ[z] = lax.fori_loop(1, NG, gp_step, gsum)
    last = pltpu.make_async_remote_copy(
        GZ.at[z], GP.at[NG], gq_s, gq_r, device_id=partner, device_id_type=MESH)
    last.start()
    last.wait_recv()
    sums = jnp.sum(GZ[z] + GP[NG], axis=1, keepdims=True)
    n0, zz, ee, qw, zw, ww, eu, uu = (sums[i:i + 1, :] for i in range(8))
    alpha0 = n0 / (damping * zz + ee)
    n1 = alpha0 * alpha0 * qw - n0
    grow = 1.0 + n1 / n0
    curve1 = (grow * grow * (damping * zz + ee) - 2.0 * grow * alpha0 * (damping * zw + eu)
              + alpha0 * alpha0 * (damping * ww + uu))
    alpha1 = n1 / curve1
    xz = alpha0 + alpha1 * grow
    xw = alpha1 * alpha0

    cv = rs_sum(1, SB[1, g]) + damping * CV[4]
    XF[0] = xz * CV[2] - xw * CV[4]
    XF[1] = CV[0] - xz * CV[3] + xw * cv

    perm = pltpu.make_async_remote_copy(
        XF, XG, pm_s, pm_r, device_id=(z, 2 * g + c), device_id_type=MESH)

    @pl.when(g != z)
    def _():
        perm.start()

    @pl.when(g == z)
    def _():
        pltpu.make_async_copy(XF, XG, pm_r).start()

    xp[...] = xz * PVEC[2] - xw * PVEC[4]
    rp[...] = PVEC[0] - xz * PVEC[3] + xw * PVEC[5]

    @pl.loop(1, NG)
    def _(d):
        zt = z_at(d)
        gt = g_at(d)
        a2a_copy(zt, zt).wait_send()
        gz_copy(zt, zt).wait_send()
        for it in range(2):
            pt_copy(it, zt, zt).wait_send()
            e_copy(it, zt, zt).wait_send()
            ag_copy(it, gt, gt).wait_send()
        for it in range(3):
            rs_copy(it, gt, gt).wait_send()
        gp_copy(gt, gt).wait_send()

    @pl.loop(0, NG)
    def _(zs):
        fwd_copy(c, zs).wait_send()
        for it in range(2):
            x_copy(it, zs).wait_send()

    last.wait_send()

    @pl.when(g != z)
    def _():
        perm.wait_send()

    pltpu.make_async_copy(XG, XG, pm_r).wait()
    for ref, i in ((xc, 0), (rc, 1)):
        for j in range(3):
            ref[0:8, j * 128:(j + 1) * 128] = XG[i, j * 8:j * 8 + 8, :]
            ref[8:9, j * 128:(j + 1) * 128] = XG[i, 24 + j:25 + j, :]


def shards(jac_point, jac_cam, resid, point_index, cam_index):
    NG = lax.axis_size("grp")
    OBS = jac_point.shape[1]
    NPTS = P_DEV
    T = NG // 2
    ROWS = T * 32
    NA = NPTS // 256
    vm = pltpu.VMEM
    dma = pltpu.SemaphoreType.DMA
    scratch = [
        vm((NG, 21, SLOT), F32), vm((2, NG, 21, SLOT), F32),
        vm((256, 2 * OBS), BF16), vm((256, OBS), BF16),
        vm((4 * ROWS, 2 * SLOT), BF16), vm((2 * NA * 8, OBS), BF16),
        vm((4 * ROWS, 256), F32), vm((1, 2 * OBS), F32), vm((1, OBS), F32),
        vm((2 * ROWS, 256), BF16), vm((NA * 8, 256), BF16),
        vm((NG, 64, 128), F32), vm((NG, 64, 128), F32),
        vm((2, NG, 32, 128), F32), vm((2, NG, 32, 128), F32),
        vm((2, NG, 32, 128), F32), vm((5, 32, 128), F32),
        vm((8, NPTS), F32), vm((6, 3, NPTS), F32),
        vm((2, NG, 1, 2 * SLOT), F32), vm((2, NG, 1, 2 * SLOT), F32),
        vm((2, 2 * NG, 1, 2 * SLOT), F32), vm((2, 2 * NG, 1, 2 * SLOT), F32),
        vm((2, 2 * NG, 1, 2 * SLOT), F32), vm((2, NG, 1, 2 * SLOT), F32),
        vm((8, 128), F32), vm((NG, 8, 128), F32), vm((NG + 1, 8, 128), F32),
        vm((2, 32, 128), F32), vm((2, 32, 128), F32),
        dma, dma((NG,)), dma((NG,)), dma((NG,)), dma((NG,)),
        dma((3, NG)), dma((3, NG)), dma((2, NG)), dma((2, NG)),
        dma((2, NG)), dma((2, NG)), dma((2, NG)), dma((2, NG)),
        dma((2, NG)), dma((2, NG)),
        dma((NG,)), dma((NG,)), dma((NG,)), dma((NG,)), dma, dma, dma, dma,
    ]
    outs = ((3, NPTS), (9, CAM_DEV), (3, NPTS), (9, CAM_DEV))
    return pl.pallas_call(
        functools.partial(kernel, NG, OBS, NPTS),
        name="cg",
        out_shape=tuple(jax.ShapeDtypeStruct(s, F32) for s in outs),
        in_specs=[pl.BlockSpec(memory_space=pltpu.VMEM)] * 5,
        out_specs=tuple(pl.BlockSpec(memory_space=pltpu.VMEM) for _ in outs),
        scratch_shapes=scratch,
        compiler_params=pltpu.CompilerParams(
            collective_id=0, has_side_effects=True, vmem_limit_bytes=48 << 20),
    )(jac_point, jac_cam, resid, point_index.reshape(1, OBS), cam_index.reshape(1, OBS))


P_DEV = 4096


def solution(mesh):
    cols, flat = P(None, ("grp", "tile")), P(("grp", "tile"))
    return jax.shard_map(
        shards, mesh=mesh, in_specs=(cols, cols, cols, flat, flat),
        out_specs=(cols,) * 4, check_vma=False)
```

```python
import functools

import jax
import jax.numpy as jnp
from jax import lax
from jax.experimental import pallas as pl
from jax.experimental.pallas import tpu as pltpu
from jax.sharding import PartitionSpec as P

F32, BF16, I32 = jnp.float32, jnp.bfloat16, jnp.int32
MESH = pl.DeviceIdType.MESH
SLOT = 256
CAM_DEV = 384
damping = 1.0


class Marks:
    def __init__(self):
        self.scope = None

    def __call__(self, name):
        if self.scope is not None:
            self.scope.__exit__(None, None, None)
        self.scope = None
        if name:
            self.scope = jax.named_scope(name)
            self.scope.__enter__()


def spread(n, d):
    half = lax.div(d + 1, jnp.int32(2))
    return half * (2 * lax.rem(d, jnp.int32(2)) - 1) + n


def kernel(
    NG, OBS, NPTS,
    jp_in, jc_in, res_in, pidx_in, cidx_in,
    xp_out, xc_out, rp_out, rc_out,
    jp, jc, res, pidx, cidx, in_s,
    S, R2, OHC, OHP, OHI, LHSI, LHS, LHSP, ACC, AROW, APROW, TV, TP,
    SB0, RB0, SB, RB, VB, CV, PV, PVEC,
    PTS, PTR, XS, XR, ER, EB, G, GS, GZ, GP, XE, XEG, XQ, XQG, XV, XG,
    loc, a2a_s, a2a_r, fwd_s, fwd_r, rs_s, rs_r, ag_s, ag_r,
    pt_s, pt_r, x_s, x_r, e_s, e_r, gz_s, gz_r, gp_s, gp_r, gq_s, gq_r, pe_s, pe_r, xp, xc, rp, rc, out_s,
):
    mark = Marks()
    moves = [pltpu.make_async_copy(a, b, in_s.at[i]) for i, (a, b) in enumerate((
        (jc_in, jc), (res_in, res), (cidx_in, cidx), (jp_in, jp), (pidx_in, pidx)))]
    for m in moves:
        m.start()
    QB = min(BLOCKS, NG)
    T = NG // 2
    ROWS = T * 32
    NA = NPTS // 256
    ng = jnp.int32(NG)
    g = lax.axis_index("grp")
    tt = lax.axis_index("tile")
    z = lax.div(tt, jnp.int32(2))
    c = lax.rem(tt, jnp.int32(2))
    partner = (g, 2 * z + 1 - c)

    two = jnp.int32(2)

    def z_at(k):
        k = jnp.int32(k)
        if NG == 16:
            far = 2 * (8 - lax.div(k - 4, two)) - 1 + jnp.where(k > 5, lax.rem(k, two), 0)
            k = jnp.where(k <= 4, k, far)
        return lax.rem(z + spread(ng, k), ng)

    def g_at(d):
        return lax.rem(g + d, ng)

    four = jnp.int32(4)

    def owner(h, k):
        d = lax.rem(k - h + ng, ng)
        if NG != 16:
            return lax.rem(h + d, ng)
        y = lax.rem(lax.div(h, four) + lax.div(d + 2, four) + 2, four)
        return 4 * y + lax.rem(h + d, four)

    def chunk_of(gg, h):
        if NG != 16:
            return gg
        y = lax.div(gg, four) - lax.div(h, four) + 4
        x = lax.rem(lax.rem(gg, four) - lax.rem(h, four) + 4, four)
        a = lax.rem(y + 2 - lax.div(x, jnp.int32(2)) + 4, four)
        return lax.rem(h + 4 * a + x, ng)

    mine_k = chunk_of(g, z)
    final = (z, 2 * mine_k + c)
    stays = jnp.logical_and(g == z, mine_k == z)

    mark("signal")
    bar = pltpu.get_barrier_semaphore()

    @pl.loop(1, NG)
    def _(d):
        pl.semaphore_signal(bar, inc=1, device_id=(g, 2 * z_at(d) + c), device_id_type=MESH)
        pl.semaphore_signal(bar, inc=1, device_id=(g_at(d), tt), device_id_type=MESH)

    pl.semaphore_signal(bar, inc=1, device_id=partner, device_id_type=MESH)

    @pl.when(jnp.logical_not(stays))
    def _():
        pl.semaphore_signal(bar, inc=1, device_id=(owner(g, z), 2 * g + c), device_id_type=MESH)

    mark("pack")
    for m in moves[:3]:
        m.wait()

    @pl.loop(0, NG)
    def _(h):
        cols = pl.ds(pl.multiple_of(h * SLOT, SLOT), SLOT)
        S[h, 0:8, :] = jc[0:8, cols]
        S[h, 8:16, :] = jc[9:17, cols]
        S[h, 16:17, :] = jc[8:9, cols]
        S[h, 17:18, :] = jc[17:18, cols]
        S[h, 18:20, :] = res[:, cols]
        S[h, 20:21, :] = cidx[:, cols].astype(F32)

    G[...] = jnp.zeros_like(G)

    mark("barrier")
    pl.semaphore_wait(bar, 2 * (NG - 1) + 1 + jnp.where(stays, 0, 1))

    def a2a_copy(zt, zf):
        return pltpu.make_async_remote_copy(
            S.at[zt], R2.at[c, zf], a2a_s.at[zt], a2a_r.at[zf],
            device_id=(g, 2 * zt + c), device_id_type=MESH)

    mark("a2a_start")
    own = pltpu.make_async_copy(S.at[z], R2.at[c, z], loc)
    own.start()

    @pl.loop(1, NG)
    def _(k):
        a2a_copy(z_at(k), z).start()

    def fold(v):
        out = v[:, 0:128]
        for i in range(1, v.shape[1] // 128):
            out = out + v[:, i * 128:(i + 1) * 128]
        return jnp.sum(out, axis=0, keepdims=True)

    def point_lhs(row0, cols, v, ap):
        v2 = jnp.concatenate([v, v], axis=0)
        low = lax.broadcasted_iota(I32, (16, SLOT), 0) < 8
        am = jnp.broadcast_to(ap, (16, SLOT)) - jnp.where(low, 0.0, 1.0)
        for i in range(NA // 2):
            LHSP[row0 + i * 16:row0 + i * 16 + 16, cols] = jnp.where(
                am == float(2 * i), v2, 0.0).astype(BF16)

    def split(v):
        hi = v.astype(BF16).astype(F32)
        return hi, v - hi

    nt = (((1,), (1,)), ((), ()))

    def point_sum(row0):
        out = lax.dot_general(LHSP[row0:row0 + NA * 8, :], OHP[...], nt,
                              preferred_element_type=F32)
        for a in range(NA):
            PV[:, a * 256:(a + 1) * 256] = out[a * 8:(a + 1) * 8, :]

    def point_gather(src, it):
        for i in range(NA // 2):
            parts = []
            for a in (2 * i, 2 * i + 1):
                hi, lo = split(PVEC[src, :, a * 256:(a + 1) * 256])
                parts += [hi, lo, jnp.zeros((2, 256), F32)]
            TP[i * 16:i * 16 + 16, :] = jnp.concatenate(parts, axis=0).astype(BF16)

        @pl.loop(0, NG // QB)
        def _(i):
            cols = pl.ds(pl.multiple_of(i * (QB * SLOT), QB * SLOT), QB * SLOT)
            got = jnp.dot(TP[...], OHP[:, cols], preferred_element_type=F32)
            ap = jnp.broadcast_to(APROW[:, cols], (8, QB * SLOT))
            acc = jnp.zeros((8, QB * SLOT), F32)
            for a in range(NA):
                acc = jnp.where(ap == float(a), got[a * 8:(a + 1) * 8, :], acc)
            v = acc[0:3] + acc[3:6]
            t0 = jnp.sum(jp[0:3, cols] * v, axis=0, keepdims=True)
            t1 = jnp.sum(jp[3:6, cols] * v, axis=0, keepdims=True)
            for b in range(QB):
                PTS[it, i * QB + b, :, 0:SLOT] = t0[:, b * SLOT:(b + 1) * SLOT]
                PTS[it, i * QB + b, :, SLOT:2 * SLOT] = t1[:, b * SLOT:(b + 1) * SLOT]

        pltpu.make_async_copy(PTS.at[it, z], PTR.at[it, z], pt_r.at[it, z]).start()

        @pl.loop(1, NG)
        def _(k):
            pt_copy(it, z_at(k), z).start()

    def pt_copy(it, zt, zf):
        return pltpu.make_async_remote_copy(
            PTS.at[it, zt], PTR.at[it, zf], pt_s.at[it, zt], pt_r.at[it, zf],
            device_id=(g, 2 * zt + c), device_id_type=MESH)

    mark("pt_init")
    for m in moves[3:]:
        m.wait()

    @pl.loop(0, NG)
    def _(h):
        cols = pl.ds(pl.multiple_of(h * SLOT, SLOT), SLOT)
        p = pidx[:, cols]
        ap = lax.shift_right_logical(p, 8).astype(F32)
        n = (p & 255).astype(F32)
        APROW[:, cols] = ap
        row = lax.broadcasted_iota(I32, (256, SLOT), 0).astype(F32)
        OHP[:, cols] = jnp.where(row == jnp.broadcast_to(n, (256, SLOT)), 1.0, 0.0).astype(BF16)
        j0, j1 = jp[0:3, cols], jp[3:6, cols]
        s0, s1 = res[0:1, cols], res[1:2, cols]
        v = jnp.concatenate(
            [-(j0 * s0 + j1 * s1), j0 * j0 + j1 * j1, jnp.zeros((2, SLOT), F32)], axis=0)
        hi, lo = split(v)
        point_lhs(0, cols, hi, ap)
        point_lhs(NA * 8, cols, lo, ap)

    mark("pt_dot")
    out = lax.dot_general(LHSP[...], OHP[...], nt, preferred_element_type=F32)
    for a in range(NA):
        PV[:, a * 256:(a + 1) * 256] = (
            out[a * 8:(a + 1) * 8, :] + out[(NA + a) * 8:(NA + a + 1) * 8, :])
    prhs = PV[0:3, :]
    pmat = PV[3:6, :] + damping
    pz = prhs / pmat
    PVEC[0] = prhs
    PVEC[1] = pmat
    PVEC[2] = pz
    G[0:1, :] += fold(prhs * pz)
    G[1:2, :] += fold(pz * pz)
    mark("pt_gather0")
    point_gather(2, 0)

    pat_row = lax.broadcasted_iota(I32, (32, SLOT), 0)
    pat = jnp.where(pat_row < 8, 0, jnp.where(
        pat_row < 16, 1, jnp.where(
            pat_row < 24, 2, jnp.where(pat_row < 27, pat_row - 24, 2000)))).astype(F32)

    def cam_lhs(ref, row0, col0, v8, v1, am, t0, nt_):
        h8, l8 = split(v8)
        h1, l1 = split(v1)
        h1 = jnp.broadcast_to(h1, (8, SLOT))
        l1 = jnp.broadcast_to(l1, (8, SLOT))
        hi = jnp.concatenate([h8, h8, h8, h1], axis=0)
        lo = jnp.concatenate([l8, l8, l8, l1], axis=0)
        for t in range(nt_):
            hit = am == float(3 * (t0 + t))
            ref[row0 + t * 32:row0 + t * 32 + 32, col0:col0 + SLOT] = (
                jnp.where(hit, hi, 0.0).astype(BF16))
            ref[row0 + nt_ * 32 + t * 32:row0 + nt_ * 32 + t * 32 + 32, col0:col0 + SLOT] = (
                jnp.where(hit, lo, 0.0).astype(BF16))

    def jac(core, zs):
        return (R2[core, zs, 0:8, :], R2[core, zs, 8:16, :],
                R2[core, zs, 16:17, :], R2[core, zs, 17:18, :])

    def block(zs):
        return pl.ds(pl.multiple_of(zs * (2 * SLOT), 2 * SLOT), 2 * SLOT)

    def half_block(zs, core):
        return pl.ds(pl.multiple_of(zs * (2 * SLOT) + core * SLOT, SLOT), SLOT)

    def fwd_copy(core, zs):
        return pltpu.make_async_remote_copy(
            R2.at[core, zs], R2.at[core, zs], fwd_s.at[zs], fwd_r.at[zs],
            device_id=partner, device_id_type=MESH)

    mark("cam_init")
    ACC[...] = jnp.zeros_like(ACC)
    own.wait()
    fwd_copy(c, z).start()
    log_t = T.bit_length() - 1

    def arrived(k):
        zn = z_at(k)
        a2a_copy(zn, zn).wait_recv()
        fwd_copy(c, zn).start()

    arrived(1)

    @pl.loop(0, NG // 2)
    def _(k):
        @pl.when(2 * k + 2 < NG)
        def _():
            arrived(2 * k + 2)
            arrived(2 * k + 3)

        tot = None
        for b in range(2):
            zs = z_at(2 * k + b)
            fwd_copy(1 - c, zs).wait_recv()
        for b in range(2):
            zs = z_at(2 * k + b)
            for core in range(2):
                idx = R2[core, zs, 20:21, :].astype(I32)
                q = lax.shift_right_logical(idx, 7)
                t = lax.shift_right_logical(q * 171, 9)
                tau = lax.shift_right_logical(t, 1)
                a = 3 * (tau & (T - 1)) + (q - 3 * t)
                a = jnp.where((t & 1) == c, a, -1000).astype(F32)
                n = (lax.shift_right_logical(tau, log_t) * 128 + (idx & 127)).astype(F32)
                AROW[:, half_block(zs, core)] = a
                row = lax.broadcasted_iota(I32, (256, SLOT), 0).astype(F32)
                oh = jnp.where(row == jnp.broadcast_to(n, (256, SLOT)), 1.0, 0.0).astype(BF16)
                OHC[:, half_block(zs, core)] = oh
                col = (2 * b + core) * SLOT
                OHI[:, col:col + SLOT] = oh
                am = jnp.broadcast_to(a, (32, SLOT)) - pat
                J0, J1, j0, j1 = jac(core, zs)
                s0, s1 = R2[core, zs, 18:19, :], R2[core, zs, 19:20, :]
                cam_lhs(LHSI, 0, col, -(J0 * s0 + J1 * s1), -(j0 * s0 + j1 * s1), am, 0, T)
                cam_lhs(LHSI, 2 * ROWS, col, J0 * J0 + J1 * J1, j0 * j0 + j1 * j1, am, 0, T)
        ACC[...] += lax.dot_general(LHSI[...], OHI[...], nt, preferred_element_type=F32)

    def rs_copy(it, gt, gf, k=0):
        if it == 2:
            src, dst = SB0.at[k], RB0.at[gf]
        else:
            src, dst = SB.at[it, k], RB.at[it, gf]
        return pltpu.make_async_remote_copy(
            src, dst, rs_s.at[it, gt], rs_r.at[it, gf],
            device_id=(gt, tt), device_id_type=MESH)

    def rs_send(it, k):
        gt = owner(z, k)

        @pl.when(gt != g)
        def _():
            rs_copy(it, gt, g, k).start()

    mark("rs_init_send")
    for half in range(2):
        lanes = slice(half * 128, half * 128 + 128)
        for t in range(T):
            for part in range(2):
                r = 2 * ROWS * part + t * 32
                SB0[half * T + t, part] = (
                    ACC[r:r + 27, lanes] + ACC[r + ROWS:r + ROWS + 27, lanes])

    @pl.loop(1, NG)
    def _(d):
        rs_send(2, chunk_of(g_at(d), z))


    def rs_sum(it, total):
        def step(d, total):
            gf = g_at(d)
            rs_copy(it, gf, gf).wait_recv()
            return total + (RB0[gf] if it == 2 else RB[it, gf])
        return lax.fori_loop(1, NG, step, total)

    mark("rs_init_wait")
    both = rs_sum(2, SB0[mine_k])
    crhs = both[0]
    cmat = both[1] + damping
    cz = crhs / cmat
    CV[0] = crhs
    CV[1] = cmat
    CV[2] = cz
    G[0:1, :] += fold(crhs * cz)
    G[1:2, :] += fold(cz * cz)

    def ag_copy(it, gt, gf):
        k = chunk_of(gf, z)
        return pltpu.make_async_remote_copy(
            VB.at[it, k], VB.at[it, k], ag_s.at[it, gt], ag_r.at[it, gf],
            device_id=(gt, tt), device_id_type=MESH)

    def gather_all(it, v):
        VB[it, mine_k] = v

        @pl.loop(1, NG)
        def _(d):
            ag_copy(it, g_at(d), g).start()

        @pl.loop(1, NG)
        def _(d):
            ag_copy(it, g_at(d), g_at(d)).wait_recv()

        for half in range(2):
            lanes = slice(half * 128, half * 128 + 128)
            for t in range(T):
                hi, lo = split(jnp.concatenate(
                    [VB[it, half * T + t], jnp.zeros((5, 128), F32)], axis=0))
                TV[t * 32:t * 32 + 32, lanes] = hi.astype(BF16)
                TV[ROWS + t * 32:ROWS + t * 32 + 32, lanes] = lo.astype(BF16)

    QW = 2 * SLOT * QB

    NC = NG // QB

    def far_first(i):
        if NC == 1:
            return i
        off = jnp.where(i == 0, 2, jnp.where(i == 1, 1, jnp.where(i == 2, 3, 0)))
        return lax.rem(lax.div(z, jnp.int32(QB)) + off, jnp.int32(NC))

    def chunk(i):
        return pl.ds(pl.multiple_of(i * QW, QW), QW)

    def x_copy(it, i):
        rows = pl.ds(2 * QB * i, 2 * QB)
        return pltpu.make_async_remote_copy(
            XS.at[it, rows], XR.at[it, rows], x_s.at[it, i], x_r.at[it, i],
            device_id=partner, device_id_type=MESH)

    def e_copy(it, zt, zf):
        return pltpu.make_async_remote_copy(
            ER.at[it, 2 * zt + c], EB.at[it, zf], e_s.at[it, zt], e_r.at[it, zf],
            device_id=(g, 2 * zt + c), device_id_type=MESH)

    def cam_errors(it):
        @pl.loop(0, NG)
        def _(zs):
            pltpu.make_async_copy(PTR.at[it, zs], PTR.at[it, zs], pt_r.at[it, zs]).wait()

        @pl.loop(0, NC)
        def _(k):
            i = far_first(k)
            got = jnp.dot(TV[...], OHC[:, chunk(i)], preferred_element_type=F32)
            for b in range(2 * QB):
                zs, core = i * QB + b // 2, b % 2
                cols = slice(b * SLOT, b * SLOT + SLOT)
                am = jnp.broadcast_to(AROW[:, half_block(zs, core)], (32, SLOT)) - pat
                acc = jnp.zeros((32, SLOT), F32)
                for t in range(T):
                    acc = jnp.where(
                        am == float(3 * t),
                        got[t * 32:t * 32 + 32, cols]
                        + got[ROWS + t * 32:ROWS + t * 32 + 32, cols], acc)
                v8 = acc[0:8] + acc[8:16] + acc[16:24]
                J0, J1, j0, j1 = jac(core, zs)
                mine = jnp.where(c == core, 1.0, 0.0)
                XS[it, 2 * zs + core, :, 0:SLOT] = (
                    jnp.sum(J0 * v8 + j0 * acc[24:32], axis=0, keepdims=True)
                    + mine * PTR[it, zs, :, 0:SLOT])
                XS[it, 2 * zs + core, :, SLOT:2 * SLOT] = (
                    jnp.sum(J1 * v8 + j1 * acc[24:32], axis=0, keepdims=True)
                    + mine * PTR[it, zs, :, SLOT:2 * SLOT])
            x_copy(it, i).start()

            @pl.when(k > 0)
            def _():
                errors_of(it, far_first(k - 1))
                errors_send(it, far_first(k - 1))

        mark("err")
        errors_of(it, far_first(jnp.int32(NC - 1)))

    def errors_of(it, i):
        x_copy(it, i).wait_recv()
        for b in range(2 * QB):
            row = 2 * QB * i + b
            ER[it, row] = XS[it, row] + XR[it, row]
        for b in range(QB):
            mine = ER[it, 2 * (i * QB + b) + c]
            if it == 0:
                G[2:3, :] += fold(mine * mine)
            else:
                before = ER[0, 2 * (i * QB + b) + c]
                G[6:7, :] += fold(mine * before)
                G[7:8, :] += fold(mine * mine)

    def errors_send(it, i):
        @pl.loop(0, QB)
        def _(b):
            zs = i * QB + b

            @pl.when(zs != z)
            def _():
                e_copy(it, zs, z).start()

            @pl.when(zs == z)
            def _():
                pltpu.make_async_copy(ER.at[it, 2 * z + c], EB.at[it, z], e_r.at[it, z]).start()

    NP = 2 if T > 1 else 1
    TH = T // NP
    RH = TH * 32
    WS = min(2 * QW, 2 * OBS)

    def cam_scatter(it):
        for part in range(NP):
            ACC[0:2 * RH, :] = jnp.zeros((2 * RH, 256), F32)

            @pl.loop(0, 2 * OBS // WS)
            def _(i):
                for b in range(WS // SLOT):
                    zs, core = i * (WS // (2 * SLOT)) + b // 2, b % 2
                    e0 = ER[it, 2 * zs + core, :, 0:SLOT]
                    e1 = ER[it, 2 * zs + core, :, SLOT:2 * SLOT]
                    J0, J1, j0, j1 = jac(core, zs)
                    am = jnp.broadcast_to(AROW[:, half_block(zs, core)], (32, SLOT)) - pat
                    cam_lhs(LHS, 0, b * SLOT, J0 * e0 + J1 * e1, j0 * e0 + j1 * e1, am,
                            part * TH, TH)
                cols = pl.ds(pl.multiple_of(i * WS, WS), WS)
                ACC[0:2 * RH, :] += lax.dot_general(
                    LHS[...], OHC[:, cols], nt, preferred_element_type=F32)

            for half in range(2):
                lanes = slice(half * 128, half * 128 + 128)
                for t in range(TH):
                    SB[it, half * T + part * TH + t] = (
                        ACC[t * 32:t * 32 + 27, lanes]
                        + ACC[RH + t * 32:RH + t * 32 + 27, lanes])

            @pl.loop(0, 2 * TH)
            def _(d):
                n = lax.rem(g + d, jnp.int32(2 * TH))
                rs_send(it, lax.div(n, jnp.int32(TH)) * T + part * TH + lax.rem(n, jnp.int32(TH)))

    def point_scatter(it):
        @pl.loop(0, NG)
        def _(k):
            h = z_at(k)
            cols = pl.ds(pl.multiple_of(h * SLOT, SLOT), SLOT)
            pltpu.make_async_copy(EB.at[it, h], EB.at[it, h], e_r.at[it, h]).wait()
            e0, e1 = EB[it, h, :, 0:SLOT], EB[it, h, :, SLOT:2 * SLOT]
            hi, lo = split(jp[0:3, cols] * e0 + jp[3:6, cols] * e1)
            v = jnp.concatenate([hi, lo, jnp.zeros((2, SLOT), F32)], axis=0)
            point_lhs(0, cols, v, APROW[:, cols])

        point_sum(0)
        return PV[0:3, :] + PV[3:6, :]

    mark("ag0")
    gather_all(0, cz)
    XE[0] = crhs
    XE[1] = cmat

    def to_final(src, dst, n):
        return pltpu.make_async_remote_copy(
            src, dst, pe_s.at[n], pe_r.at[n], device_id=final, device_id_type=MESH)

    def final_start(src, dst, n):
        @pl.when(jnp.logical_not(stays))
        def _():
            to_final(src, dst, n).start()

        @pl.when(stays)
        def _():
            pltpu.make_async_copy(src, dst, pe_r.at[n]).start()

    final_start(XE, XEG, 0)
    mark("terms0")
    cam_errors(0)
    errors_send(0, far_first(jnp.int32(NC - 1)))

    mark("scat0")
    cam_scatter(0)
    mark("pscat0")
    pq = point_scatter(0) + damping * PVEC[2]
    pw = pq / PVEC[1]
    PVEC[3] = pq
    PVEC[4] = pw
    mark("pt_gather1")
    point_gather(4, 1)
    G[3:4, :] += fold(pq * pw)
    G[4:5, :] += fold(PVEC[2] * pw)
    G[5:6, :] += fold(pw * pw)

    mark("rs0_wait")
    cq = rs_sum(0, SB[0, mine_k]) + damping * CV[2]
    cw = cq / CV[1]
    CV[3] = cq
    CV[4] = cw
    G[3:4, :] += fold(cq * cw)
    G[4:5, :] += fold(CV[2] * cw)
    G[5:6, :] += fold(cw * cw)
    XQ[...] = cq
    mark("ag1")
    gather_all(1, cw)
    final_start(XQ, XQG, 1)
    mark("terms1")
    cam_errors(1)

    def gz_copy(zt, zf):
        return pltpu.make_async_remote_copy(
            GS, GZ.at[zf], gz_s.at[zt], gz_r.at[zf],
            device_id=(g, 2 * zt + c), device_id_type=MESH)

    def gp_copy(gt, gf):
        return pltpu.make_async_remote_copy(
            GP.at[gf], GP.at[gf], gp_s.at[gt], gp_r.at[gf],
            device_id=(gt, tt), device_id_type=MESH)

    lane = lax.broadcasted_iota(I32, (8, 128), 1)
    row8 = lax.broadcasted_iota(I32, (8, 128), 0)
    each = jnp.broadcast_to(jnp.sum(G[...], axis=1, keepdims=True), (8, 128))
    mine = jnp.sum(jnp.where(lane == row8, each, 0.0), axis=0, keepdims=True)
    GS[...] = mine

    @pl.loop(1, NG)
    def _(k):
        gz_copy(z_at(k), z).start()

    errors_send(1, far_first(jnp.int32(NC - 1)))
    mark("scat1")
    cam_scatter(1)
    mark("pscat1")
    PVEC[5] = point_scatter(1) + damping * PVEC[4]
    mark("gram_z")

    def gz_step(k, total):
        zs = z_at(k)
        gz_copy(zs, zs).wait_recv()
        return total + GZ[zs]

    gsum = lax.fori_loop(1, NG, gz_step, mine)
    GP[g] = gsum

    @pl.loop(1, NG)
    def _(d):
        gp_copy(g_at(d), g).start()

    mark("rs1_wait")
    XV[...] = rs_sum(1, SB[1, mine_k]) + damping * CV[4]
    mark("perm")
    final_start(XV, XG, 2)
    mark("gram_p")

    def gp_step(d, total):
        gf = g_at(d)
        gp_copy(gf, gf).wait_recv()
        return total + GP[gf]

    GZ[z] = lax.fori_loop(1, NG, gp_step, gsum)
    last = pltpu.make_async_remote_copy(
        GZ.at[z], GP.at[NG], gq_s, gq_r, device_id=partner, device_id_type=MESH)
    last.start()
    last.wait_recv()
    mark("final")
    total = GZ[z] + GP[NG]
    n0, zz, ee, qw, zw, ww, eu, uu = (total[:, i:i + 1] for i in range(8))
    alpha0 = n0 / (damping * zz + ee)
    n1 = alpha0 * alpha0 * qw - n0
    grow = 1.0 + n1 / n0
    curve1 = (grow * grow * (damping * zz + ee) - 2.0 * grow * alpha0 * (damping * zw + eu)
              + alpha0 * alpha0 * (damping * ww + uu))
    alpha1 = n1 / curve1
    xz = alpha0 + alpha1 * grow
    xw = alpha1 * alpha0

    xp[...] = xz * PVEC[2] - xw * PVEC[4]
    rp[...] = PVEC[0] - xz * PVEC[3] + xw * PVEC[5]
    results = [pltpu.make_async_copy(a, b, out_s.at[i]) for i, (a, b) in enumerate((
        (xp, xp_out), (rp, rp_out), (xc, xc_out), (rc, rc_out)))]
    results[0].start()
    results[1].start()

    def put(ref, v):
        for j in range(3):
            ref[0:8, j * 128:(j + 1) * 128] = v[j * 8:j * 8 + 8, :]
            ref[8:9, j * 128:(j + 1) * 128] = v[24 + j:25 + j, :]

    pltpu.make_async_copy(XEG, XEG, pe_r.at[0]).wait()
    pltpu.make_async_copy(XQG, XQG, pe_r.at[1]).wait()
    put(xc, (xz * XEG[0] - xw * XQG[...]) / XEG[1])
    results[2].start()
    base = XEG[0] - xz * XQG[...]

    mark("sends")
    @pl.loop(1, NG)
    def _(d):
        zt = z_at(d)
        gt = g_at(d)
        a2a_copy(zt, zt).wait_send()
        gz_copy(zt, zt).wait_send()
        for it in range(2):
            pt_copy(it, zt, zt).wait_send()
            e_copy(it, zt, zt).wait_send()
            ag_copy(it, gt, gt).wait_send()
        for it in range(3):
            rs_copy(it, gt, gt).wait_send()
        gp_copy(gt, gt).wait_send()

    @pl.loop(0, NG)
    def _(zs):
        fwd_copy(c, zs).wait_send()

    @pl.loop(0, NG // QB)
    def _(i):
        for it in range(2):
            x_copy(it, i).wait_send()

    last.wait_send()

    @pl.when(jnp.logical_not(stays))
    def _():
        to_final(XE, XEG, 0).wait_send()
        to_final(XQ, XQG, 1).wait_send()
        to_final(XV, XG, 2).wait_send()

    mark("perm_wait")
    pltpu.make_async_copy(XG, XG, pe_r.at[2]).wait()
    put(rc, base + xw * XG[...])
    results[3].start()
    for m in results:
        m.wait()
    mark(None)


def shards(jac_point, jac_cam, resid, point_index, cam_index):
    NG = lax.axis_size("grp")
    OBS = jac_point.shape[1]
    NPTS = P_DEV
    T = NG // 2
    ROWS = T * 32
    NA = NPTS // 256
    vm = pltpu.VMEM
    dma = pltpu.SemaphoreType.DMA
    QB = min(BLOCKS, NG)
    scratch = [
        vm((6, OBS), F32), vm((18, OBS), F32), vm((2, OBS), F32),
        vm((1, OBS), I32), vm((1, OBS), I32), dma((5,)),
        vm((NG, 21, SLOT), F32), vm((2, NG, 21, SLOT), F32),
        vm((256, 2 * OBS), BF16), vm((256, OBS), BF16),
        vm((256, 4 * SLOT), BF16), vm((4 * ROWS, 4 * SLOT), BF16),
        vm((2 * ROWS // min(2, T), min(4 * SLOT * QB, 2 * OBS)), BF16), vm((2 * NA * 8, OBS), BF16),
        vm((4 * ROWS, 256), F32), vm((1, 2 * OBS), F32), vm((1, OBS), F32),
        vm((2 * ROWS, 256), BF16), vm((NA * 8, 256), BF16),
        vm((NG, 2, 27, 128), F32), vm((NG, 2, 27, 128), F32),
        vm((2, NG, 27, 128), F32), vm((2, NG, 27, 128), F32),
        vm((2, NG, 27, 128), F32), vm((5, 27, 128), F32),
        vm((8, NPTS), F32), vm((6, 3, NPTS), F32),
        vm((2, NG, 1, 2 * SLOT), F32), vm((2, NG, 1, 2 * SLOT), F32),
        vm((2, 2 * NG, 1, 2 * SLOT), F32), vm((2, 2 * NG, 1, 2 * SLOT), F32),
        vm((2, 2 * NG, 1, 2 * SLOT), F32), vm((2, NG, 1, 2 * SLOT), F32),
        vm((8, 128), F32), vm((1, 128), F32),
        vm((NG, 1, 128), F32), vm((NG + 1, 1, 128), F32),
        vm((2, 27, 128), F32), vm((2, 27, 128), F32),
        vm((27, 128), F32), vm((27, 128), F32),
        vm((27, 128), F32), vm((27, 128), F32),
        dma, dma((NG,)), dma((NG,)), dma((NG,)), dma((NG,)),
        dma((3, NG)), dma((3, NG)), dma((2, NG)), dma((2, NG)),
        dma((2, NG)), dma((2, NG)), dma((2, NG // QB)), dma((2, NG // QB)),
        dma((2, NG)), dma((2, NG)),
        dma((NG,)), dma((NG,)), dma((NG,)), dma((NG,)), dma, dma, dma((3,)), dma((3,)),
    ]
    outs = ((3, NPTS), (9, CAM_DEV), (3, NPTS), (9, CAM_DEV))
    made = pl.pallas_call(
        functools.partial(kernel, NG, OBS, NPTS),
        name="cg",
        out_shape=tuple(jax.ShapeDtypeStruct(s, F32) for s in outs),
        in_specs=[pl.BlockSpec(memory_space=pltpu.HBM)] * 5,
        out_specs=tuple(pl.BlockSpec(memory_space=pltpu.HBM) for _ in outs),
        scratch_shapes=scratch + [vm(s, F32) for s in outs] + [dma((4,))],
        compiler_params=pltpu.CompilerParams(
            collective_id=0, has_side_effects=True, vmem_limit_bytes=VMEM_ALL),
    )(jac_point, jac_cam, resid, point_index.reshape(1, OBS), cam_index.reshape(1, OBS))
    return pl.pallas_call(
        store,
        name="store",
        out_shape=tuple(jax.ShapeDtypeStruct(s, F32) for s in outs),
        in_specs=[pl.BlockSpec(memory_space=pltpu.HBM)] * 4,
        out_specs=tuple(pl.BlockSpec(memory_space=pltpu.HBM) for _ in outs),
        scratch_shapes=[vm(s, F32) for s in outs] + [dma((4,)), dma((4,))],
        compiler_params=pltpu.CompilerParams(vmem_limit_bytes=VMEM_ALL),
    )(*made)


def store(*refs):
    got, sent = refs[12], refs[13]
    loads = [pltpu.make_async_copy(refs[i], refs[8 + i], got.at[i]) for i in range(4)]
    stores = [pltpu.make_async_copy(refs[8 + i], refs[4 + i], sent.at[i]) for i in range(4)]
    for m in loads:
        m.start()
    for i in range(4):
        loads[i].wait()
        stores[i].start()
    for m in stores:
        m.wait()


P_DEV = 4096
VMEM_ALL = 67043328
BLOCKS = 4


def solution(mesh):
    cols, flat = P(None, ("grp", "tile")), P(("grp", "tile"))
    return jax.shard_map(
        shards, mesh=mesh, in_specs=(cols, cols, cols, flat, flat),
        out_specs=(cols,) * 4, check_vma=False)
```

```python
import functools

import jax
import jax.numpy as jnp
from jax import lax
from jax.experimental import pallas as pl
from jax.experimental.pallas import tpu as pltpu
from jax.sharding import PartitionSpec as P

F32, BF16, I32 = jnp.float32, jnp.bfloat16, jnp.int32
MESH = pl.DeviceIdType.MESH
SLOT = 256
CAM_DEV = 384
damping = 1.0


class Marks:
    def __init__(self):
        self.scope = None

    def __call__(self, name):
        if self.scope is not None:
            self.scope.__exit__(None, None, None)
        self.scope = None
        if name:
            self.scope = jax.named_scope(name)
            self.scope.__enter__()


def spread(n, d):
    half = lax.div(d + 1, jnp.int32(2))
    return half * (2 * lax.rem(d, jnp.int32(2)) - 1) + n


def kernel(
    NG, OBS, NPTS,
    jp_in, jc_in, res_in, pidx_in, cidx_in,
    xp_out, xc_out, rp_out, rc_out,
    jp, jc, res, pidx, cidx, in_s,
    S, R2, OHC, OHP, OHI, LHSI, LHS, LHSP, ACC, AROW, APROW, TV, TP,
    LHSF, SB, RB, VB, CV, PV, PVEC,
    PTS, PTR, XS, XR, ER, EB, G, GS, GZ, GP, XE, XEG, XQ, XQG, XV, XG,
    loc, a2a_s, a2a_r, fwd_s, fwd_r, rs_s, rs_r, ag_s, ag_r,
    pt_s, pt_r, x_s, x_r, e_s, e_r, gz_s, gz_r, gp_s, gp_r, gq_s, gq_r, pe_s, pe_r, xp, xc, rp, rc, out_s,
):
    mark = Marks()
    moves = [pltpu.make_async_copy(a, b, in_s.at[i]) for i, (a, b) in enumerate((
        (jc_in, jc), (res_in, res), (cidx_in, cidx), (jp_in, jp), (pidx_in, pidx)))]
    for m in moves:
        m.start()
    QB = min(BLOCKS, NG)
    T = NG // 2
    ROWS = T * 32
    NA = NPTS // 256
    ng = jnp.int32(NG)
    g = lax.axis_index("grp")
    tt = lax.axis_index("tile")
    z = lax.div(tt, jnp.int32(2))
    c = lax.rem(tt, jnp.int32(2))
    partner = (g, 2 * z + 1 - c)

    two = jnp.int32(2)

    def z_at(k):
        k = jnp.int32(k)
        if NG == 16:
            far = 2 * (8 - lax.div(k - 4, two)) - 1 + jnp.where(k > 5, lax.rem(k, two), 0)
            k = jnp.where(k <= 4, k, far)
        return lax.rem(z + spread(ng, k), ng)

    def g_at(d):
        return lax.rem(g + d, ng)

    four = jnp.int32(4)

    def owner(h, k):
        d = lax.rem(k - h + ng, ng)
        if NG != 16:
            return lax.rem(h + d, ng)
        y = lax.rem(lax.div(h, four) + lax.div(d + 2, four) + 2, four)
        return 4 * y + lax.rem(h + d, four)

    def chunk_of(gg, h):
        if NG != 16:
            return gg
        y = lax.div(gg, four) - lax.div(h, four) + 4
        x = lax.rem(lax.rem(gg, four) - lax.rem(h, four) + 4, four)
        a = lax.rem(y + 2 - lax.div(x, jnp.int32(2)) + 4, four)
        return lax.rem(h + 4 * a + x, ng)

    mine_k = chunk_of(g, z)
    final = (z, 2 * mine_k + c)
    stays = jnp.logical_and(g == z, mine_k == z)

    def take(ref, sem):
        pltpu.make_async_copy(ref, ref, sem).wait()

    mark("signal")
    bar = pltpu.get_barrier_semaphore()

    @pl.loop(1, NG)
    def _(d):
        pl.semaphore_signal(bar, inc=1, device_id=(g, 2 * z_at(d) + c), device_id_type=MESH)
        pl.semaphore_signal(bar, inc=1, device_id=(g_at(d), tt), device_id_type=MESH)

    pl.semaphore_signal(bar, inc=1, device_id=partner, device_id_type=MESH)

    @pl.when(jnp.logical_not(stays))
    def _():
        pl.semaphore_signal(bar, inc=1, device_id=(owner(g, z), 2 * g + c), device_id_type=MESH)

    mark("pack")
    for m in moves[:3]:
        m.wait()

    @pl.loop(0, NG)
    def _(h):
        cols = pl.ds(pl.multiple_of(h * SLOT, SLOT), SLOT)
        S[h, 0:8, :] = jc[0:8, cols]
        S[h, 8:16, :] = jc[9:17, cols]
        S[h, 16:17, :] = jc[8:9, cols]
        S[h, 17:18, :] = jc[17:18, cols]
        S[h, 18:20, :] = res[:, cols]
        S[h, 20:21, :] = cidx[:, cols].astype(F32)

    G[...] = jnp.zeros_like(G)

    mark("barrier")
    pl.semaphore_wait(bar, 2 * (NG - 1) + 1 + jnp.where(stays, 0, 1))

    def a2a_copy(zt, zf):
        return pltpu.make_async_remote_copy(
            S.at[zt], R2.at[c, zf], a2a_s, a2a_r.at[zf],
            device_id=(g, 2 * zt + c), device_id_type=MESH)

    mark("a2a_start")
    own = pltpu.make_async_copy(S.at[z], R2.at[c, z], loc)
    own.start()

    @pl.loop(1, NG)
    def _(k):
        a2a_copy(z_at(k), z).start()

    def fold(v):
        out = v[:, 0:128]
        for i in range(1, v.shape[1] // 128):
            out = out + v[:, i * 128:(i + 1) * 128]
        return jnp.sum(out, axis=0, keepdims=True)

    def point_lhs(row0, cols, v, ap):
        v2 = jnp.concatenate([v, v], axis=0)
        low = lax.broadcasted_iota(I32, (16, SLOT), 0) < 8
        am = jnp.broadcast_to(ap, (16, SLOT)) - jnp.where(low, 0.0, 1.0)
        for i in range(NA // 2):
            LHSP[row0 + i * 16:row0 + i * 16 + 16, cols] = jnp.where(
                am == float(2 * i), v2, 0.0).astype(BF16)

    def split(v):
        hi = v.astype(BF16).astype(F32)
        return hi, v - hi

    nt = (((1,), (1,)), ((), ()))

    def point_sum(row0):
        out = lax.dot_general(LHSP[row0:row0 + NA * 8, :], OHP[...], nt,
                              preferred_element_type=F32)
        for a in range(NA):
            PV[:, a * 256:(a + 1) * 256] = out[a * 8:(a + 1) * 8, :]

    def point_gather(src, it):
        for i in range(NA // 2):
            parts = []
            for a in (2 * i, 2 * i + 1):
                hi, lo = split(PVEC[src, :, a * 256:(a + 1) * 256])
                parts += [hi, lo, jnp.zeros((2, 256), F32)]
            TP[i * 16:i * 16 + 16, :] = jnp.concatenate(parts, axis=0).astype(BF16)

        @pl.loop(0, NG // QB)
        def _(i):
            cols = pl.ds(pl.multiple_of(i * (QB * SLOT), QB * SLOT), QB * SLOT)
            got = jnp.dot(TP[...], OHP[:, cols], preferred_element_type=F32)
            ap = jnp.broadcast_to(APROW[:, cols], (8, QB * SLOT))
            acc = jnp.zeros((8, QB * SLOT), F32)
            for a in range(NA):
                acc = jnp.where(ap == float(a), got[a * 8:(a + 1) * 8, :], acc)
            v = acc[0:3] + acc[3:6]
            t0 = jnp.sum(jp[0:3, cols] * v, axis=0, keepdims=True)
            t1 = jnp.sum(jp[3:6, cols] * v, axis=0, keepdims=True)
            for b in range(QB):
                PTS[it, i * QB + b, :, 0:SLOT] = t0[:, b * SLOT:(b + 1) * SLOT]
                PTS[it, i * QB + b, :, SLOT:2 * SLOT] = t1[:, b * SLOT:(b + 1) * SLOT]

        pltpu.make_async_copy(
            PTS.at[it, z], PTR.at[it, z], pt_r.at[it, lax.div(z, jnp.int32(QB))]).start()

        @pl.loop(1, NG)
        def _(k):
            pt_copy(it, z_at(k), z).start()

    def pt_copy(it, zt, zf):
        return pltpu.make_async_remote_copy(
            PTS.at[it, zt], PTR.at[it, zf], pt_s.at[it], pt_r.at[it, lax.div(zf, jnp.int32(QB))],
            device_id=(g, 2 * zt + c), device_id_type=MESH)

    mark("pt_init")
    for m in moves[3:]:
        m.wait()

    @pl.loop(0, NG)
    def _(h):
        cols = pl.ds(pl.multiple_of(h * SLOT, SLOT), SLOT)
        p = pidx[:, cols]
        ap = lax.shift_right_logical(p, 8).astype(F32)
        n = (p & 255).astype(F32)
        APROW[:, cols] = ap
        row = lax.broadcasted_iota(I32, (256, SLOT), 0).astype(F32)
        OHP[:, cols] = jnp.where(row == jnp.broadcast_to(n, (256, SLOT)), 1.0, 0.0).astype(BF16)
        j0, j1 = jp[0:3, cols], jp[3:6, cols]
        s0, s1 = res[0:1, cols], res[1:2, cols]
        v = jnp.concatenate(
            [-(j0 * s0 + j1 * s1), j0 * j0 + j1 * j1, jnp.zeros((2, SLOT), F32)], axis=0)
        hi, lo = split(v)
        point_lhs(0, cols, hi, ap)
        point_lhs(NA * 8, cols, lo, ap)

    mark("pt_dot")
    out = lax.dot_general(LHSP[...], OHP[...], nt, preferred_element_type=F32)
    for a in range(NA):
        PV[:, a * 256:(a + 1) * 256] = (
            out[a * 8:(a + 1) * 8, :] + out[(NA + a) * 8:(NA + a + 1) * 8, :])
    prhs = PV[0:3, :]
    pmat = PV[3:6, :] + damping
    pz = prhs / pmat
    PVEC[0] = prhs
    PVEC[1] = pmat
    PVEC[2] = pz
    G[0:1, :] += fold(prhs * pz)
    G[1:2, :] += fold(pz * pz)
    mark("pt_gather0")
    point_gather(2, 0)

    pat_row = lax.broadcasted_iota(I32, (32, SLOT), 0)
    pat = jnp.where(pat_row < 8, 0, jnp.where(
        pat_row < 16, 1, jnp.where(
            pat_row < 24, 2, jnp.where(pat_row < 27, pat_row - 24, 2000)))).astype(F32)

    def cam_lhs(ref, row0, col0, v8, v1, am, nt_):
        h8, l8 = split(v8)
        h1, l1 = split(v1)
        h1 = jnp.broadcast_to(h1, (8, SLOT))
        l1 = jnp.broadcast_to(l1, (8, SLOT))
        hi = jnp.concatenate([h8, h8, h8, h1], axis=0)
        lo = jnp.concatenate([l8, l8, l8, l1], axis=0)
        for t in range(nt_):
            hit = am == float(3 * t)
            ref[row0 + t * 32:row0 + t * 32 + 32, col0:col0 + SLOT] = (
                jnp.where(hit, hi, 0.0).astype(BF16))
            ref[row0 + nt_ * 32 + t * 32:row0 + nt_ * 32 + t * 32 + 32, col0:col0 + SLOT] = (
                jnp.where(hit, lo, 0.0).astype(BF16))

    def jac(core, zs):
        return (R2[core, zs, 0:8, :], R2[core, zs, 8:16, :],
                R2[core, zs, 16:17, :], R2[core, zs, 17:18, :])

    def block(zs):
        return pl.ds(pl.multiple_of(zs * (2 * SLOT), 2 * SLOT), 2 * SLOT)

    def half_block(zs, core):
        return pl.ds(pl.multiple_of(zs * (2 * SLOT) + core * SLOT, SLOT), SLOT)

    def fwd_copy(core, zs):
        return pltpu.make_async_remote_copy(
            R2.at[core, zs], R2.at[core, zs], fwd_s, fwd_r.at[zs],
            device_id=partner, device_id_type=MESH)

    mark("cam_init")
    ACC[...] = jnp.zeros_like(ACC)
    own.wait()
    fwd_copy(c, z).start()
    log_t = T.bit_length() - 1

    def arrived(k):
        zn = z_at(k)
        a2a_copy(zn, zn).wait_recv()
        fwd_copy(c, zn).start()

    FB = min(6, NG // 2)
    LB = NG - FB

    def indices(zs, core, col):
        idx = R2[core, zs, 20:21, :].astype(I32)
        q = lax.shift_right_logical(idx, 7)
        t = lax.shift_right_logical(q * 171, 9)
        tau = lax.shift_right_logical(t, 1)
        a = 3 * (tau & (T - 1)) + (q - 3 * t)
        a = jnp.where((t & 1) == c, a, -1000).astype(F32)
        n = (lax.shift_right_logical(tau, log_t) * 128 + (idx & 127)).astype(F32)
        AROW[:, half_block(zs, core)] = a
        row = lax.broadcasted_iota(I32, (256, SLOT), 0).astype(F32)
        oh = jnp.where(row == jnp.broadcast_to(n, (256, SLOT)), 1.0, 0.0).astype(BF16)
        OHC[:, half_block(zs, core)] = oh
        OHI[:, col:col + SLOT] = oh
        return a

    arrived(1)

    @pl.loop(0, LB // 2)
    def _(k):
        arrived(2 * k + 2)
        arrived(2 * k + 3)
        for b in range(2):
            fwd_copy(1 - c, z_at(2 * k + b)).wait_recv()
        for b in range(2):
            zs = z_at(2 * k + b)
            for core in range(2):
                col = (2 * b + core) * SLOT
                am = jnp.broadcast_to(indices(zs, core, col), (32, SLOT)) - pat
                J0, J1, j0, j1 = jac(core, zs)
                s0, s1 = R2[core, zs, 18:19, :], R2[core, zs, 19:20, :]
                cam_lhs(LHSI, 0, col, -(J0 * s0 + J1 * s1), -(j0 * s0 + j1 * s1), am, T)
                cam_lhs(LHSI, 2 * ROWS, col, J0 * J0 + J1 * J1, j0 * j0 + j1 * j1, am, T)
        ACC[...] += lax.dot_general(
            LHSI[...], OHI[:, 0:4 * SLOT], nt, preferred_element_type=F32)

    def rs_copy(it, gt, gf, k=0):
        return pltpu.make_async_remote_copy(
            SB.at[it, k], RB.at[it, gf], rs_s.at[it], rs_r.at[it],
            device_id=(gt, tt), device_id_type=MESH)

    def rs_send(it, k):
        gt = owner(z, k)

        @pl.when(gt != g)
        def _():
            rs_copy(it, gt, g, k).start()

    @pl.loop(LB + 2, NG)
    def _(k):
        arrived(k)

    @pl.loop(LB, NG)
    def _(k):
        fwd_copy(1 - c, z_at(k)).wait_recv()

    mark("cam_last")
    for b in range(2 * FB):
        indices(z_at(LB + b // 2), b % 2, b * SLOT)

    @pl.loop(0, 2)
    def _(part):
        rhs = part == 0
        for b in range(2 * FB):
            zs, core = z_at(LB + b // 2), b % 2
            J0, J1, j0, j1 = jac(core, zs)
            s0, s1 = R2[core, zs, 18:19, :], R2[core, zs, 19:20, :]
            f0 = jnp.where(rhs, jnp.broadcast_to(-s0, (8, SLOT)), J0)
            f1 = jnp.where(rhs, jnp.broadcast_to(-s1, (8, SLOT)), J1)
            g0 = jnp.where(rhs, -s0, j0)
            g1 = jnp.where(rhs, -s1, j1)
            am = jnp.broadcast_to(AROW[:, half_block(zs, core)], (32, SLOT)) - pat
            cam_lhs(LHSF, 0, b * SLOT, J0 * f0 + J1 * f1, j0 * g0 + j1 * g1, am, T)
        top = pl.multiple_of(part * (2 * ROWS), 2 * ROWS)
        both = ACC[pl.ds(top, 2 * ROWS), :] + lax.dot_general(
            LHSF[...], OHI[:, 0:2 * FB * SLOT], nt, preferred_element_type=F32)
        for half in range(2):
            lanes = slice(half * 128, half * 128 + 128)
            for t in range(T):
                SB[2 + part, half * T + t] = (
                    both[t * 32:t * 32 + 27, lanes]
                    + both[ROWS + t * 32:ROWS + t * 32 + 27, lanes])

        @pl.loop(1, NG)
        def _(d):
            rs_send(2 + part, chunk_of(g_at(d), z))

    mark("rs_init_wait")

    def rs_sum(it, total):
        others = pl.ds(0, NG - 1)
        take(RB.at[it, others], rs_r.at[it])

        def step(d, total):
            gf = g_at(d)
            return total + RB[it, gf]
        return lax.fori_loop(1, NG, step, total)

    mark("rs_init_wait")
    crhs = rs_sum(2, SB[2, mine_k])
    cmat = rs_sum(3, SB[3, mine_k]) + damping
    cz = crhs / cmat
    CV[0] = crhs
    CV[1] = cmat
    CV[2] = cz
    G[0:1, :] += fold(crhs * cz)
    G[1:2, :] += fold(cz * cz)

    def ag_copy(it, gt, gf):
        k = chunk_of(gf, z)
        return pltpu.make_async_remote_copy(
            VB.at[it, k], VB.at[it, k], ag_s.at[it], ag_r.at[it],
            device_id=(gt, tt), device_id_type=MESH)

    def gather_all(it, v):
        VB[it, mine_k] = v

        @pl.loop(1, NG)
        def _(d):
            ag_copy(it, g_at(d), g).start()

        take(VB.at[it, pl.ds(0, NG - 1)], ag_r.at[it])

        for half in range(2):
            lanes = slice(half * 128, half * 128 + 128)
            for t in range(T):
                hi, lo = split(jnp.concatenate(
                    [VB[it, half * T + t], jnp.zeros((5, 128), F32)], axis=0))
                TV[t * 32:t * 32 + 32, lanes] = hi.astype(BF16)
                TV[ROWS + t * 32:ROWS + t * 32 + 32, lanes] = lo.astype(BF16)

    QW = 2 * SLOT * QB

    NC = NG // QB

    def order(it, k):
        if NC == 1:
            return jnp.int32(0)
        side = jnp.where(k == 1, 1, 3)
        ends = (2, 0) if it == 0 else (0, 2)
        off = jnp.where(k == 0, ends[0], jnp.where(k == 3, ends[1], side))
        return lax.rem(lax.div(z, jnp.int32(QB)) + off, jnp.int32(NC))

    def chunk(i):
        return pl.ds(pl.multiple_of(i * QW, QW), QW)

    def x_copy(it, i):
        rows = pl.ds(2 * QB * i, 2 * QB)
        return pltpu.make_async_remote_copy(
            XS.at[it, rows], XR.at[it, rows], x_s.at[it], x_r.at[it, i],
            device_id=partner, device_id_type=MESH)

    def e_copy(it, zt, zf):
        return pltpu.make_async_remote_copy(
            ER.at[it, 2 * zt + c], EB.at[it, zf], e_s.at[it], e_r.at[it],
            device_id=(g, 2 * zt + c), device_id_type=MESH)

    def cam_errors(it):
        @pl.loop(0, NC)
        def _(k):
            i = order(it, k)
            take(PTR.at[it, pl.ds(i * QB, QB)], pt_r.at[it, i])
            got = jnp.dot(TV[...], OHC[:, chunk(i)], preferred_element_type=F32)
            for b in range(2 * QB):
                zs, core = i * QB + b // 2, b % 2
                cols = slice(b * SLOT, b * SLOT + SLOT)
                am = jnp.broadcast_to(AROW[:, half_block(zs, core)], (32, SLOT)) - pat
                acc = jnp.zeros((32, SLOT), F32)
                for t in range(T):
                    acc = jnp.where(
                        am == float(3 * t),
                        got[t * 32:t * 32 + 32, cols]
                        + got[ROWS + t * 32:ROWS + t * 32 + 32, cols], acc)
                v8 = acc[0:8] + acc[8:16] + acc[16:24]
                J0, J1, j0, j1 = jac(core, zs)
                mine = jnp.where(c == core, 1.0, 0.0)
                XS[it, 2 * zs + core, :, 0:SLOT] = (
                    jnp.sum(J0 * v8 + j0 * acc[24:32], axis=0, keepdims=True)
                    + mine * PTR[it, zs, :, 0:SLOT])
                XS[it, 2 * zs + core, :, SLOT:2 * SLOT] = (
                    jnp.sum(J1 * v8 + j1 * acc[24:32], axis=0, keepdims=True)
                    + mine * PTR[it, zs, :, SLOT:2 * SLOT])
            x_copy(it, i).start()

            @pl.when(k > 0)
            def _():
                errors_of(it, order(it, k - 1))
                errors_send(it, order(it, k - 1))

    def errors_of(it, i):
        x_copy(it, i).wait_recv()
        for b in range(2 * QB):
            row = 2 * QB * i + b
            ER[it, row] = XS[it, row] + XR[it, row]
        for b in range(QB):
            mine = ER[it, 2 * (i * QB + b) + c]
            if it == 0:
                G[2:3, :] += fold(mine * mine)
            else:
                before = ER[0, 2 * (i * QB + b) + c]
                G[6:7, :] += fold(mine * before)
                G[7:8, :] += fold(mine * mine)

    def errors_send(it, i):
        @pl.loop(0, QB)
        def _(b):
            zs = i * QB + b

            @pl.when(zs != z)
            def _():
                e_copy(it, zs, z).start()

            @pl.when(zs == z)
            def _():
                pltpu.make_async_copy(ER.at[it, 2 * z + c], EB.at[it, z], e_r.at[it]).start()

    NP = 2 if T > 1 else 1
    TH = T // NP
    RH = TH * 32
    WS = min(2 * QW, 2 * OBS)

    def gz_copy(zt, zf):
        return pltpu.make_async_remote_copy(
            GS, GZ.at[zf], gz_s, gz_r,
            device_id=(g, 2 * zt + c), device_id_type=MESH)

    def last_errors(it):
        errors_of(it, order(it, jnp.int32(NC - 1)))
        if it == 1:
            lane = lax.broadcasted_iota(I32, (8, 128), 1)
            row8 = lax.broadcasted_iota(I32, (8, 128), 0)
            each = jnp.broadcast_to(jnp.sum(G[...], axis=1, keepdims=True), (8, 128))
            GS[...] = jnp.sum(jnp.where(lane == row8, each, 0.0), axis=0, keepdims=True)

            @pl.loop(1, NG)
            def _(k):
                gz_copy(z_at(k), z).start()

        errors_send(it, order(it, jnp.int32(NC - 1)))

    def cam_scatter(it):
        steps = 2 * OBS // WS
        tail = order(it, jnp.int32(NC - 1))

        @pl.loop(0, NP * steps)
        def _(n):
            if steps == 1:
                part, first, last, i = n, True, True, jnp.int32(0)

                @pl.when(n == 0)
                def _():
                    last_errors(it)
            else:
                part, turn = lax.div(n, jnp.int32(2)), lax.rem(n, jnp.int32(2))
                first, last = turn == 0, turn == 1
                i = lax.rem(lax.div(tail, jnp.int32(2)) + 1 + turn, jnp.int32(2))

                @pl.when(n == 1)
                def _():
                    last_errors(it)

            shift = pat + (3 * TH * part).astype(F32)
            for b in range(WS // SLOT):
                zs, core = i * (WS // (2 * SLOT)) + b // 2, b % 2
                e0 = ER[it, 2 * zs + core, :, 0:SLOT]
                e1 = ER[it, 2 * zs + core, :, SLOT:2 * SLOT]
                J0, J1, j0, j1 = jac(core, zs)
                am = jnp.broadcast_to(AROW[:, half_block(zs, core)], (32, SLOT)) - shift
                cam_lhs(LHS, 0, b * SLOT, J0 * e0 + J1 * e1, j0 * e0 + j1 * e1, am, TH)
            cols = pl.ds(pl.multiple_of(i * WS, WS), WS)
            got = lax.dot_general(LHS[...], OHC[:, cols], nt, preferred_element_type=F32)
            ACC[0:2 * RH, :] = got + jnp.where(first, 0.0, ACC[0:2 * RH, :])

            @pl.when(last)
            def _():
                for half in range(2):
                    lanes = slice(half * 128, half * 128 + 128)
                    for t in range(TH):
                        SB[it, half * T + part * TH + t] = (
                            ACC[t * 32:t * 32 + 27, lanes]
                            + ACC[RH + t * 32:RH + t * 32 + 27, lanes])

                @pl.loop(0, 2 * TH)
                def _(d):
                    m = lax.rem(g + d, jnp.int32(2 * TH))
                    rs_send(it, lax.div(m, jnp.int32(TH)) * T + part * TH
                            + lax.rem(m, jnp.int32(TH)))

    def point_scatter(it):
        take(EB.at[it], e_r.at[it])

        @pl.loop(0, NG)
        def _(k):
            h = z_at(k)
            cols = pl.ds(pl.multiple_of(h * SLOT, SLOT), SLOT)
            e0, e1 = EB[it, h, :, 0:SLOT], EB[it, h, :, SLOT:2 * SLOT]
            hi, lo = split(jp[0:3, cols] * e0 + jp[3:6, cols] * e1)
            v = jnp.concatenate([hi, lo, jnp.zeros((2, SLOT), F32)], axis=0)
            point_lhs(0, cols, v, APROW[:, cols])

        point_sum(0)
        return PV[0:3, :] + PV[3:6, :]

    mark("ag0")
    gather_all(0, cz)
    XE[0] = crhs
    XE[1] = cmat

    def to_final(src, dst, n):
        return pltpu.make_async_remote_copy(
            src, dst, pe_s.at[n], pe_r.at[n], device_id=final, device_id_type=MESH)

    def final_start(src, dst, n):
        @pl.when(jnp.logical_not(stays))
        def _():
            to_final(src, dst, n).start()

        @pl.when(stays)
        def _():
            pltpu.make_async_copy(src, dst, pe_r.at[n]).start()

    final_start(XE, XEG, 0)
    mark("terms0")
    cam_errors(0)
    mark("scat0")
    cam_scatter(0)
    mark("pscat0")
    pq = point_scatter(0) + damping * PVEC[2]
    pw = pq / PVEC[1]
    PVEC[3] = pq
    PVEC[4] = pw
    mark("pt_gather1")
    point_gather(4, 1)
    G[3:4, :] += fold(pq * pw)
    G[4:5, :] += fold(PVEC[2] * pw)
    G[5:6, :] += fold(pw * pw)

    mark("rs0_wait")
    cq = rs_sum(0, SB[0, mine_k]) + damping * CV[2]
    cw = cq / CV[1]
    CV[3] = cq
    CV[4] = cw
    G[3:4, :] += fold(cq * cw)
    G[4:5, :] += fold(CV[2] * cw)
    G[5:6, :] += fold(cw * cw)
    XQ[...] = cq
    mark("ag1")
    gather_all(1, cw)
    final_start(XQ, XQG, 1)
    mark("terms1")
    cam_errors(1)

    def gp_copy(gt, gf):
        return pltpu.make_async_remote_copy(
            GP.at[gf], GP.at[gf], gp_s, gp_r,
            device_id=(gt, tt), device_id_type=MESH)

    mark("scat1")
    cam_scatter(1)
    mark("rs1_wait")
    XV[...] = rs_sum(1, SB[1, mine_k]) + damping * CV[4]
    mark("perm")
    final_start(XV, XG, 2)
    mark("gram_z")

    def gz_step(k, total):
        return total + GZ[z_at(k)]

    take(GZ.at[pl.ds(0, NG - 1)], gz_r)
    gsum = lax.fori_loop(1, NG, gz_step, GS[...])
    GP[g] = gsum

    @pl.loop(1, NG)
    def _(d):
        gp_copy(g_at(d), g).start()

    mark("pscat1")
    PVEC[5] = point_scatter(1) + damping * PVEC[4]

    mark("gram_p")

    def gp_step(d, total):
        return total + GP[g_at(d)]

    take(GP.at[pl.ds(0, NG - 1)], gp_r)
    GZ[z] = lax.fori_loop(1, NG, gp_step, gsum)
    last = pltpu.make_async_remote_copy(
        GZ.at[z], GP.at[NG], gq_s, gq_r, device_id=partner, device_id_type=MESH)
    last.start()
    last.wait_recv()
    mark("final")
    total = GZ[z] + GP[NG]
    n0, zz, ee, qw, zw, ww, eu, uu = (total[:, i:i + 1] for i in range(8))
    alpha0 = n0 / (damping * zz + ee)
    n1 = alpha0 * alpha0 * qw - n0
    grow = 1.0 + n1 / n0
    curve1 = (grow * grow * (damping * zz + ee) - 2.0 * grow * alpha0 * (damping * zw + eu)
              + alpha0 * alpha0 * (damping * ww + uu))
    alpha1 = n1 / curve1
    xz = alpha0 + alpha1 * grow
    xw = alpha1 * alpha0

    xp[...] = xz * PVEC[2] - xw * PVEC[4]
    rp[...] = PVEC[0] - xz * PVEC[3] + xw * PVEC[5]
    results = [pltpu.make_async_copy(a, b, out_s.at[i]) for i, (a, b) in enumerate((
        (xp, xp_out), (rp, rp_out), (xc, xc_out), (rc, rc_out)))]
    results[0].start()
    results[1].start()

    def put(ref, v):
        for j in range(3):
            ref[0:8, j * 128:(j + 1) * 128] = v[j * 8:j * 8 + 8, :]
            ref[8:9, j * 128:(j + 1) * 128] = v[24 + j:25 + j, :]

    pltpu.make_async_copy(XEG, XEG, pe_r.at[0]).wait()
    pltpu.make_async_copy(XQG, XQG, pe_r.at[1]).wait()
    put(xc, (xz * XEG[0] - xw * XQG[...]) / XEG[1])
    results[2].start()
    base = XEG[0] - xz * XQG[...]

    mark("sends")
    others = pl.ds(0, NG - 1)
    take(S.at[others], a2a_s)
    take(R2.at[c], fwd_s)
    take(SB.at[2, others], rs_s.at[2])
    take(SB.at[3, others], rs_s.at[3])
    for it in range(2):
        take(SB.at[it, others], rs_s.at[it])
        take(VB.at[it, others], ag_s.at[it])
        take(PTS.at[it, others], pt_s.at[it])
        take(XS.at[it], x_s.at[it])
        take(ER.at[it, others], e_s.at[it])
    take(GZ.at[others], gz_s)
    take(GP.at[others], gp_s)
    last.wait_send()

    @pl.when(jnp.logical_not(stays))
    def _():
        to_final(XE, XEG, 0).wait_send()
        to_final(XQ, XQG, 1).wait_send()
        to_final(XV, XG, 2).wait_send()

    mark("perm_wait")
    pltpu.make_async_copy(XG, XG, pe_r.at[2]).wait()
    put(rc, base + xw * XG[...])
    results[3].start()
    for m in results:
        m.wait()
    mark(None)


def shards(jac_point, jac_cam, resid, point_index, cam_index):
    NG = lax.axis_size("grp")
    OBS = jac_point.shape[1]
    NPTS = P_DEV
    T = NG // 2
    ROWS = T * 32
    NA = NPTS // 256
    vm = pltpu.VMEM
    dma = pltpu.SemaphoreType.DMA
    QB = min(BLOCKS, NG)
    scratch = [
        vm((6, OBS), F32), vm((18, OBS), F32), vm((2, OBS), F32),
        vm((1, OBS), I32), vm((1, OBS), I32), dma((5,)),
        vm((NG, 21, SLOT), F32), vm((2, NG, 21, SLOT), F32),
        vm((256, 2 * OBS), BF16), vm((256, OBS), BF16),
        vm((256, max(4, 2 * min(6, NG // 2)) * SLOT), BF16),
        vm((4 * ROWS, 4 * SLOT), BF16),
        vm((2 * ROWS // min(2, T), min(4 * SLOT * QB, 2 * OBS)), BF16), vm((2 * NA * 8, OBS), BF16),
        vm((4 * ROWS, 256), F32), vm((1, 2 * OBS), F32), vm((1, OBS), F32),
        vm((2 * ROWS, 256), BF16), vm((NA * 8, 256), BF16),
        vm((2 * ROWS, 2 * min(6, NG // 2) * SLOT), BF16),
        vm((4, NG, 27, 128), F32), vm((4, NG, 27, 128), F32),
        vm((2, NG, 27, 128), F32), vm((5, 27, 128), F32),
        vm((8, NPTS), F32), vm((6, 3, NPTS), F32),
        vm((2, NG, 1, 2 * SLOT), F32), vm((2, NG, 1, 2 * SLOT), F32),
        vm((2, 2 * NG, 1, 2 * SLOT), F32), vm((2, 2 * NG, 1, 2 * SLOT), F32),
        vm((2, 2 * NG, 1, 2 * SLOT), F32), vm((2, NG, 1, 2 * SLOT), F32),
        vm((8, 128), F32), vm((1, 128), F32),
        vm((NG, 1, 128), F32), vm((NG + 1, 1, 128), F32),
        vm((2, 27, 128), F32), vm((2, 27, 128), F32),
        vm((27, 128), F32), vm((27, 128), F32),
        vm((27, 128), F32), vm((27, 128), F32),
        dma, dma, dma((NG,)), dma, dma((NG,)),
        dma((4,)), dma((4,)), dma((2,)), dma((2,)),
        dma((2,)), dma((2, NG // QB)), dma((2,)), dma((2, NG // QB)),
        dma((2,)), dma((2,)), dma, dma, dma, dma,
        dma, dma, dma((3,)), dma((3,)),
    ]
    outs = ((3, NPTS), (9, CAM_DEV), (3, NPTS), (9, CAM_DEV))
    made = pl.pallas_call(
        functools.partial(kernel, NG, OBS, NPTS),
        name="cg",
        out_shape=tuple(jax.ShapeDtypeStruct(s, F32) for s in outs),
        in_specs=[pl.BlockSpec(memory_space=pltpu.HBM)] * 5,
        out_specs=tuple(pl.BlockSpec(memory_space=pltpu.HBM) for _ in outs),
        scratch_shapes=scratch + [vm(s, F32) for s in outs] + [dma((4,))],
        compiler_params=pltpu.CompilerParams(
            collective_id=0, has_side_effects=True, vmem_limit_bytes=VMEM_ALL),
    )(jac_point, jac_cam, resid, point_index.reshape(1, OBS), cam_index.reshape(1, OBS))
    return pl.pallas_call(
        store,
        name="store",
        out_shape=tuple(jax.ShapeDtypeStruct(s, F32) for s in outs),
        in_specs=[pl.BlockSpec(memory_space=pltpu.HBM)] * 4,
        out_specs=tuple(pl.BlockSpec(memory_space=pltpu.HBM) for _ in outs),
        scratch_shapes=[vm(s, F32) for s in outs] + [dma((4,)), dma((4,))],
        compiler_params=pltpu.CompilerParams(vmem_limit_bytes=VMEM_ALL),
    )(*made)


def store(*refs):
    got, sent = refs[12], refs[13]
    loads = [pltpu.make_async_copy(refs[i], refs[8 + i], got.at[i]) for i in range(4)]
    stores = [pltpu.make_async_copy(refs[8 + i], refs[4 + i], sent.at[i]) for i in range(4)]
    for m in loads:
        m.start()
    for i in range(4):
        loads[i].wait()
        stores[i].start()
    for m in stores:
        m.wait()


P_DEV = 4096
VMEM_ALL = 67043328
BLOCKS = 4


def solution(mesh):
    cols, flat = P(None, ("grp", "tile")), P(("grp", "tile"))
    return jax.shard_map(
        shards, mesh=mesh, in_specs=(cols, cols, cols, flat, flat),
        out_specs=(cols,) * 4, check_vma=False)
```

```python
import functools

import jax
import jax.numpy as jnp
from jax import lax
from jax.experimental import pallas as pl
from jax.experimental.pallas import tpu as pltpu
from jax.sharding import PartitionSpec as P

F32, BF16, I32 = jnp.float32, jnp.bfloat16, jnp.int32
MESH = pl.DeviceIdType.MESH
SLOT = 256
CAM_DEV = 384
damping = 1.0


class Marks:
    def __init__(self):
        self.scope = None

    def __call__(self, name):
        if self.scope is not None:
            self.scope.__exit__(None, None, None)
        self.scope = None
        if name:
            self.scope = jax.named_scope(name)
            self.scope.__enter__()


def spread(n, d):
    half = lax.div(d + 1, jnp.int32(2))
    return half * (2 * lax.rem(d, jnp.int32(2)) - 1) + n


def kernel(
    NG, OBS, NPTS,
    jp_in, jc_in, res_in, pidx_in, cidx_in,
    xp_out, xc_out, rp_out, rc_out,
    jp, jc, res, pidx, cidx, in_s,
    S, R2, OHC, OHP, OHI, LHSI, LHS, LHSP, ACC, AROW, APROW, TV, TP,
    LHSF, SB, RB, VB, CV, PV, PVEC,
    PTS, PTR, XS, XR, ER, EB, G, GS, GZ, GP, XE, XEG, XQ, XQG, XV, XG,
    loc, a2a_s, a2a_r, fwd_s, fwd_r, rs_s, rs_r, ag_s, ag_r,
    pt_s, pt_r, x_s, x_r, e_s, e_r, gz_s, gz_r, gp_s, gp_r, pe_s, pe_r, xp, xc, rp, rc, out_s,
):
    mark = Marks()
    moves = [pltpu.make_async_copy(a, b, in_s.at[i]) for i, (a, b) in enumerate((
        (jc_in, jc), (res_in, res), (cidx_in, cidx), (jp_in, jp), (pidx_in, pidx)))]
    for m in moves:
        m.start()
    QB = min(BLOCKS, NG)
    T = NG // 2
    ROWS = T * 32
    NA = NPTS // 256
    ng = jnp.int32(NG)
    g = lax.axis_index("grp")
    tt = lax.axis_index("tile")
    z = lax.div(tt, jnp.int32(2))
    c = lax.rem(tt, jnp.int32(2))
    partner = (g, 2 * z + 1 - c)

    two = jnp.int32(2)

    def z_at(k):
        k = jnp.int32(k)
        if NG == 16:
            far = 2 * (8 - lax.div(k - 4, two)) - 1 + jnp.where(k > 5, lax.rem(k, two), 0)
            k = jnp.where(k <= 4, k, far)
        return lax.rem(z + spread(ng, k), ng)

    def g_at(d):
        return lax.rem(g + d, ng)

    four = jnp.int32(4)

    def owner(h, k):
        d = lax.rem(k - h + ng, ng)
        if NG != 16:
            return lax.rem(h + d, ng)
        y = lax.rem(lax.div(h, four) + lax.div(d + 2, four) + 2, four)
        return 4 * y + lax.rem(h + d, four)

    def chunk_of(gg, h):
        if NG != 16:
            return gg
        y = lax.div(gg, four) - lax.div(h, four) + 4
        x = lax.rem(lax.rem(gg, four) - lax.rem(h, four) + 4, four)
        a = lax.rem(y + 2 - lax.div(x, jnp.int32(2)) + 4, four)
        return lax.rem(h + 4 * a + x, ng)

    mine_k = chunk_of(g, z)
    final = (z, 2 * mine_k + c)
    stays = jnp.logical_and(g == z, mine_k == z)

    def take(ref, sem):
        pltpu.make_async_copy(ref, ref, sem).wait()

    mark("signal")
    bar = pltpu.get_barrier_semaphore()

    @pl.loop(1, NG)
    def _(d):
        zf = lax.rem(z + spread(ng, ng - d), ng)
        pl.semaphore_signal(bar, inc=1, device_id=(g, 2 * zf + c), device_id_type=MESH)

    @pl.loop(1, NG)
    def _(d):
        pl.semaphore_signal(bar, inc=1, device_id=(g_at(d), tt), device_id_type=MESH)
        pl.semaphore_signal(bar, inc=1, device_id=(g_at(d), 2 * z + 1 - c), device_id_type=MESH)

    pl.semaphore_signal(bar, inc=1, device_id=partner, device_id_type=MESH)

    @pl.when(jnp.logical_not(stays))
    def _():
        pl.semaphore_signal(bar, inc=1, device_id=(owner(g, z), 2 * g + c), device_id_type=MESH)

    mark("pack")
    for m in moves[:3]:
        m.wait()

    @pl.loop(0, NG)
    def _(h):
        cols = pl.ds(pl.multiple_of(h * SLOT, SLOT), SLOT)
        S[h, 0:8, :] = jc[0:8, cols]
        S[h, 8:16, :] = jc[9:17, cols]
        S[h, 16:17, :] = jc[8:9, cols]
        S[h, 17:18, :] = jc[17:18, cols]
        S[h, 18:20, :] = res[:, cols]
        S[h, 20:21, :] = cidx[:, cols].astype(F32)

    G[...] = jnp.zeros_like(G)

    mark("barrier")
    pl.semaphore_wait(bar, 3 * (NG - 1) + 1 + jnp.where(stays, 0, 1))

    def a2a_copy(zt, zf):
        return pltpu.make_async_remote_copy(
            S.at[zt], R2.at[c, zf], a2a_s, a2a_r.at[zf],
            device_id=(g, 2 * zt + c), device_id_type=MESH)

    mark("a2a_start")
    own = pltpu.make_async_copy(S.at[z], R2.at[c, z], loc)
    own.start()

    @pl.loop(1, NG)
    def _(k):
        a2a_copy(z_at(k), z).start()

    def fold(v):
        out = v[:, 0:128]
        for i in range(1, v.shape[1] // 128):
            out = out + v[:, i * 128:(i + 1) * 128]
        return jnp.sum(out, axis=0, keepdims=True)

    def point_lhs(row0, cols, v, ap):
        v2 = jnp.concatenate([v, v], axis=0)
        low = lax.broadcasted_iota(I32, (16, SLOT), 0) < 8
        am = jnp.broadcast_to(ap, (16, SLOT)) - jnp.where(low, 0.0, 1.0)
        for i in range(NA // 2):
            LHSP[row0 + i * 16:row0 + i * 16 + 16, cols] = jnp.where(
                am == float(2 * i), v2, 0.0).astype(BF16)

    def split(v):
        hi = v.astype(BF16).astype(F32)
        return hi, v - hi

    nt = (((1,), (1,)), ((), ()))

    def point_sum(row0):
        out = lax.dot_general(LHSP[row0:row0 + NA * 8, :], OHP[...], nt,
                              preferred_element_type=F32)
        for a in range(NA):
            PV[:, a * 256:(a + 1) * 256] = out[a * 8:(a + 1) * 8, :]

    def point_gather(src, it):
        for i in range(NA // 2):
            parts = []
            for a in (2 * i, 2 * i + 1):
                hi, lo = split(PVEC[src, :, a * 256:(a + 1) * 256])
                parts += [hi, lo, jnp.zeros((2, 256), F32)]
            TP[i * 16:i * 16 + 16, :] = jnp.concatenate(parts, axis=0).astype(BF16)

        @pl.loop(0, NG // QB)
        def _(i):
            cols = pl.ds(pl.multiple_of(i * (QB * SLOT), QB * SLOT), QB * SLOT)
            got = jnp.dot(TP[...], OHP[:, cols], preferred_element_type=F32)
            ap = jnp.broadcast_to(APROW[:, cols], (8, QB * SLOT))
            acc = jnp.zeros((8, QB * SLOT), F32)
            for a in range(NA):
                acc = jnp.where(ap == float(a), got[a * 8:(a + 1) * 8, :], acc)
            v = acc[0:3] + acc[3:6]
            t0 = jnp.sum(jp[0:3, cols] * v, axis=0, keepdims=True)
            t1 = jnp.sum(jp[3:6, cols] * v, axis=0, keepdims=True)
            for b in range(QB):
                PTS[it, i * QB + b, :, 0:SLOT] = t0[:, b * SLOT:(b + 1) * SLOT]
                PTS[it, i * QB + b, :, SLOT:2 * SLOT] = t1[:, b * SLOT:(b + 1) * SLOT]

        pltpu.make_async_copy(
            PTS.at[it, z], PTR.at[it, z], pt_r.at[it, lax.div(z, jnp.int32(QB))]).start()

        @pl.loop(1, NG)
        def _(k):
            pt_copy(it, z_at(k), z).start()

    def pt_copy(it, zt, zf):
        return pltpu.make_async_remote_copy(
            PTS.at[it, zt], PTR.at[it, zf], pt_s.at[it], pt_r.at[it, lax.div(zf, jnp.int32(QB))],
            device_id=(g, 2 * zt + c), device_id_type=MESH)

    mark("pt_init")
    for m in moves[3:]:
        m.wait()

    @pl.loop(0, NG)
    def _(h):
        cols = pl.ds(pl.multiple_of(h * SLOT, SLOT), SLOT)
        p = pidx[:, cols]
        ap = lax.shift_right_logical(p, 8).astype(F32)
        n = (p & 255).astype(F32)
        APROW[:, cols] = ap
        row = lax.broadcasted_iota(I32, (256, SLOT), 0).astype(F32)
        OHP[:, cols] = jnp.where(row == jnp.broadcast_to(n, (256, SLOT)), 1.0, 0.0).astype(BF16)
        j0, j1 = jp[0:3, cols], jp[3:6, cols]
        s0, s1 = res[0:1, cols], res[1:2, cols]
        v = jnp.concatenate(
            [-(j0 * s0 + j1 * s1), j0 * j0 + j1 * j1, jnp.zeros((2, SLOT), F32)], axis=0)
        hi, lo = split(v)
        point_lhs(0, cols, hi, ap)
        point_lhs(NA * 8, cols, lo, ap)

    mark("pt_dot")
    out = lax.dot_general(LHSP[...], OHP[...], nt, preferred_element_type=F32)
    for a in range(NA):
        PV[:, a * 256:(a + 1) * 256] = (
            out[a * 8:(a + 1) * 8, :] + out[(NA + a) * 8:(NA + a + 1) * 8, :])
    prhs = PV[0:3, :]
    pmat = PV[3:6, :] + damping
    pz = prhs / pmat
    PVEC[0] = prhs
    PVEC[1] = pmat
    PVEC[2] = pz
    G[0:1, :] += fold(prhs * pz)
    G[1:2, :] += fold(pz * pz)
    mark("pt_gather0")
    point_gather(2, 0)

    pat_row = lax.broadcasted_iota(I32, (32, SLOT), 0)
    pat = jnp.where(pat_row < 8, 0, jnp.where(
        pat_row < 16, 1, jnp.where(
            pat_row < 24, 2, jnp.where(pat_row < 27, pat_row - 24, 2000)))).astype(F32)

    def cam_lhs(ref, row0, col0, v8, v1, am, nt_):
        h8, l8 = split(v8)
        h1, l1 = split(v1)
        h1 = jnp.broadcast_to(h1, (8, SLOT))
        l1 = jnp.broadcast_to(l1, (8, SLOT))
        hi = jnp.concatenate([h8, h8, h8, h1], axis=0)
        lo = jnp.concatenate([l8, l8, l8, l1], axis=0)
        for t in range(nt_):
            hit = am == float(3 * t)
            ref[row0 + t * 32:row0 + t * 32 + 32, col0:col0 + SLOT] = (
                jnp.where(hit, hi, 0.0).astype(BF16))
            ref[row0 + nt_ * 32 + t * 32:row0 + nt_ * 32 + t * 32 + 32, col0:col0 + SLOT] = (
                jnp.where(hit, lo, 0.0).astype(BF16))

    def jac(core, zs):
        return (R2[core, zs, 0:8, :], R2[core, zs, 8:16, :],
                R2[core, zs, 16:17, :], R2[core, zs, 17:18, :])

    def block(zs):
        return pl.ds(pl.multiple_of(zs * (2 * SLOT), 2 * SLOT), 2 * SLOT)

    def half_block(zs, core):
        return pl.ds(pl.multiple_of(zs * (2 * SLOT) + core * SLOT, SLOT), SLOT)

    def fwd_copy(core, zs):
        return pltpu.make_async_remote_copy(
            R2.at[core, zs], R2.at[core, zs], fwd_s, fwd_r.at[zs],
            device_id=partner, device_id_type=MESH)

    mark("cam_init")
    ACC[...] = jnp.zeros_like(ACC)
    own.wait()
    fwd_copy(c, z).start()
    log_t = T.bit_length() - 1

    def arrived(k):
        zn = z_at(k)
        a2a_copy(zn, zn).wait_recv()
        fwd_copy(c, zn).start()

    FB = min(6, NG // 2)
    LB = NG - FB

    def indices(zs, core, col):
        idx = R2[core, zs, 20:21, :].astype(I32)
        q = lax.shift_right_logical(idx, 7)
        t = lax.shift_right_logical(q * 171, 9)
        tau = lax.shift_right_logical(t, 1)
        a = 3 * (tau & (T - 1)) + (q - 3 * t)
        a = jnp.where((t & 1) == c, a, -1000).astype(F32)
        n = (lax.shift_right_logical(tau, log_t) * 128 + (idx & 127)).astype(F32)
        AROW[:, half_block(zs, core)] = a
        row = lax.broadcasted_iota(I32, (256, SLOT), 0).astype(F32)
        oh = jnp.where(row == jnp.broadcast_to(n, (256, SLOT)), 1.0, 0.0).astype(BF16)
        OHC[:, half_block(zs, core)] = oh
        OHI[:, col:col + SLOT] = oh
        return a

    arrived(1)

    @pl.loop(0, LB // 2)
    def _(k):
        arrived(2 * k + 2)
        arrived(2 * k + 3)
        for b in range(2):
            fwd_copy(1 - c, z_at(2 * k + b)).wait_recv()
        for b in range(2):
            zs = z_at(2 * k + b)
            for core in range(2):
                col = (2 * b + core) * SLOT
                am = jnp.broadcast_to(indices(zs, core, col), (32, SLOT)) - pat
                J0, J1, j0, j1 = jac(core, zs)
                s0, s1 = R2[core, zs, 18:19, :], R2[core, zs, 19:20, :]
                cam_lhs(LHSI, 0, col, -(J0 * s0 + J1 * s1), -(j0 * s0 + j1 * s1), am, T)
                cam_lhs(LHSI, 2 * ROWS, col, J0 * J0 + J1 * J1, j0 * j0 + j1 * j1, am, T)
        ACC[...] += lax.dot_general(
            LHSI[...], OHI[:, 0:4 * SLOT], nt, preferred_element_type=F32)

    def rs_copy(it, gt, gf, k=0):
        return pltpu.make_async_remote_copy(
            SB.at[it, k], RB.at[it, gf], rs_s.at[it], rs_r.at[it],
            device_id=(gt, tt), device_id_type=MESH)

    def rs_send(it, k):
        gt = owner(z, k)

        @pl.when(gt != g)
        def _():
            rs_copy(it, gt, g, k).start()

    @pl.loop(LB + 2, NG)
    def _(k):
        arrived(k)

    @pl.loop(LB, NG)
    def _(k):
        fwd_copy(1 - c, z_at(k)).wait_recv()

    mark("cam_last")
    for b in range(2 * FB):
        indices(z_at(LB + b // 2), b % 2, b * SLOT)

    @pl.loop(0, 2)
    def _(part):
        rhs = part == 0
        for b in range(2 * FB):
            zs, core = z_at(LB + b // 2), b % 2
            J0, J1, j0, j1 = jac(core, zs)
            s0, s1 = R2[core, zs, 18:19, :], R2[core, zs, 19:20, :]
            f0 = jnp.where(rhs, jnp.broadcast_to(-s0, (8, SLOT)), J0)
            f1 = jnp.where(rhs, jnp.broadcast_to(-s1, (8, SLOT)), J1)
            g0 = jnp.where(rhs, -s0, j0)
            g1 = jnp.where(rhs, -s1, j1)
            am = jnp.broadcast_to(AROW[:, half_block(zs, core)], (32, SLOT)) - pat
            cam_lhs(LHSF, 0, b * SLOT, J0 * f0 + J1 * f1, j0 * g0 + j1 * g1, am, T)
        top = pl.multiple_of(part * (2 * ROWS), 2 * ROWS)
        both = ACC[pl.ds(top, 2 * ROWS), :] + lax.dot_general(
            LHSF[...], OHI[:, 0:2 * FB * SLOT], nt, preferred_element_type=F32)
        for half in range(2):
            lanes = slice(half * 128, half * 128 + 128)
            for t in range(T):
                SB[2 + part, half * T + t] = (
                    both[t * 32:t * 32 + 27, lanes]
                    + both[ROWS + t * 32:ROWS + t * 32 + 27, lanes])

        @pl.loop(1, NG)
        def _(d):
            rs_send(2 + part, chunk_of(g_at(d), z))

    mark("rs_init_wait")

    def rs_sum(it, total):
        others = pl.ds(0, NG - 1)
        take(RB.at[it, others], rs_r.at[it])

        def step(d, total):
            gf = g_at(d)
            return total + RB[it, gf]
        return lax.fori_loop(1, NG, step, total)

    mark("rs_init_wait")
    crhs = rs_sum(2, SB[2, mine_k])
    cmat = rs_sum(3, SB[3, mine_k]) + damping
    cz = crhs / cmat
    CV[0] = crhs
    CV[1] = cmat
    CV[2] = cz
    G[0:1, :] += fold(crhs * cz)
    G[1:2, :] += fold(cz * cz)

    def ag_copy(it, gt, gf):
        k = chunk_of(gf, z)
        return pltpu.make_async_remote_copy(
            VB.at[it, k], VB.at[it, k], ag_s.at[it], ag_r.at[it],
            device_id=(gt, tt), device_id_type=MESH)

    def gather_all(it, v):
        VB[it, mine_k] = v

        @pl.loop(1, NG)
        def _(d):
            ag_copy(it, g_at(d), g).start()

        take(VB.at[it, pl.ds(0, NG - 1)], ag_r.at[it])

        for half in range(2):
            lanes = slice(half * 128, half * 128 + 128)
            for t in range(T):
                hi, lo = split(jnp.concatenate(
                    [VB[it, half * T + t], jnp.zeros((5, 128), F32)], axis=0))
                TV[t * 32:t * 32 + 32, lanes] = hi.astype(BF16)
                TV[ROWS + t * 32:ROWS + t * 32 + 32, lanes] = lo.astype(BF16)

    QW = 2 * SLOT * QB

    NC = NG // QB

    def order(it, k):
        if NC == 1:
            return jnp.int32(0)
        side = jnp.where(k == 1, 1, 3)
        ends = (2, 0) if it == 0 else (0, 2)
        off = jnp.where(k == 0, ends[0], jnp.where(k == 3, ends[1], side))
        return lax.rem(lax.div(z, jnp.int32(QB)) + off, jnp.int32(NC))

    def chunk(i):
        return pl.ds(pl.multiple_of(i * QW, QW), QW)

    def x_copy(it, i):
        rows = pl.ds(2 * QB * i, 2 * QB)
        return pltpu.make_async_remote_copy(
            XS.at[it, rows], XR.at[it, rows], x_s.at[it], x_r.at[it, i],
            device_id=partner, device_id_type=MESH)

    def e_copy(it, zt, zf):
        return pltpu.make_async_remote_copy(
            ER.at[it, 2 * zt + c], EB.at[it, zf], e_s.at[it], e_r.at[it],
            device_id=(g, 2 * zt + c), device_id_type=MESH)

    def cam_errors(it):
        @pl.loop(0, NC)
        def _(k):
            i = order(it, k)
            take(PTR.at[it, pl.ds(i * QB, QB)], pt_r.at[it, i])
            got = jnp.dot(TV[...], OHC[:, chunk(i)], preferred_element_type=F32)
            for b in range(2 * QB):
                zs, core = i * QB + b // 2, b % 2
                cols = slice(b * SLOT, b * SLOT + SLOT)
                am = jnp.broadcast_to(AROW[:, half_block(zs, core)], (32, SLOT)) - pat
                acc = jnp.zeros((32, SLOT), F32)
                for t in range(T):
                    acc = jnp.where(
                        am == float(3 * t),
                        got[t * 32:t * 32 + 32, cols]
                        + got[ROWS + t * 32:ROWS + t * 32 + 32, cols], acc)
                v8 = acc[0:8] + acc[8:16] + acc[16:24]
                J0, J1, j0, j1 = jac(core, zs)
                mine = jnp.where(c == core, 1.0, 0.0)
                XS[it, 2 * zs + core, :, 0:SLOT] = (
                    jnp.sum(J0 * v8 + j0 * acc[24:32], axis=0, keepdims=True)
                    + mine * PTR[it, zs, :, 0:SLOT])
                XS[it, 2 * zs + core, :, SLOT:2 * SLOT] = (
                    jnp.sum(J1 * v8 + j1 * acc[24:32], axis=0, keepdims=True)
                    + mine * PTR[it, zs, :, SLOT:2 * SLOT])
            x_copy(it, i).start()

            @pl.when(k > 0)
            def _():
                errors_of(it, order(it, k - 1))
                errors_send(it, order(it, k - 1))

    def errors_of(it, i):
        x_copy(it, i).wait_recv()
        for b in range(2 * QB):
            row = 2 * QB * i + b
            ER[it, row] = XS[it, row] + XR[it, row]
        for b in range(QB):
            mine = ER[it, 2 * (i * QB + b) + c]
            if it == 0:
                G[2:3, :] += fold(mine * mine)
            else:
                before = ER[0, 2 * (i * QB + b) + c]
                G[6:7, :] += fold(mine * before)
                G[7:8, :] += fold(mine * mine)

    def errors_send(it, i):
        @pl.loop(0, QB)
        def _(b):
            zs = i * QB + b

            @pl.when(zs != z)
            def _():
                e_copy(it, zs, z).start()

            @pl.when(zs == z)
            def _():
                pltpu.make_async_copy(ER.at[it, 2 * z + c], EB.at[it, z], e_r.at[it]).start()

    NP = 2 if T > 1 else 1
    TH = T // NP
    RH = TH * 32
    WS = min(2 * QW, 2 * OBS)

    def gz_copy(zt, zf):
        return pltpu.make_async_remote_copy(
            GS, GZ.at[zf], gz_s, gz_r,
            device_id=(g, 2 * zt + c), device_id_type=MESH)

    def last_errors(it):
        errors_of(it, order(it, jnp.int32(NC - 1)))
        if it == 1:
            lane = lax.broadcasted_iota(I32, (8, 128), 1)
            row8 = lax.broadcasted_iota(I32, (8, 128), 0)
            each = jnp.broadcast_to(jnp.sum(G[...], axis=1, keepdims=True), (8, 128))
            GS[...] = jnp.sum(jnp.where(lane == row8, each, 0.0), axis=0, keepdims=True)

            @pl.loop(1, NG)
            def _(k):
                gz_copy(z_at(k), z).start()

        errors_send(it, order(it, jnp.int32(NC - 1)))

    def cam_scatter(it):
        steps = 2 * OBS // WS
        tail = order(it, jnp.int32(NC - 1))

        @pl.loop(0, NP * steps)
        def _(n):
            if steps == 1:
                part, first, last, i = n, True, True, jnp.int32(0)

                @pl.when(n == 0)
                def _():
                    last_errors(it)
            else:
                part, turn = lax.div(n, jnp.int32(2)), lax.rem(n, jnp.int32(2))
                first, last = turn == 0, turn == 1
                i = lax.rem(lax.div(tail, jnp.int32(2)) + 1 + turn, jnp.int32(2))

                @pl.when(n == 1)
                def _():
                    last_errors(it)

            shift = pat + (3 * TH * part).astype(F32)
            for b in range(WS // SLOT):
                zs, core = i * (WS // (2 * SLOT)) + b // 2, b % 2
                e0 = ER[it, 2 * zs + core, :, 0:SLOT]
                e1 = ER[it, 2 * zs + core, :, SLOT:2 * SLOT]
                J0, J1, j0, j1 = jac(core, zs)
                am = jnp.broadcast_to(AROW[:, half_block(zs, core)], (32, SLOT)) - shift
                cam_lhs(LHS, 0, b * SLOT, J0 * e0 + J1 * e1, j0 * e0 + j1 * e1, am, TH)
            cols = pl.ds(pl.multiple_of(i * WS, WS), WS)
            got = lax.dot_general(LHS[...], OHC[:, cols], nt, preferred_element_type=F32)
            ACC[0:2 * RH, :] = got + jnp.where(first, 0.0, ACC[0:2 * RH, :])

            @pl.when(last)
            def _():
                for half in range(2):
                    lanes = slice(half * 128, half * 128 + 128)
                    for t in range(TH):
                        SB[it, half * T + part * TH + t] = (
                            ACC[t * 32:t * 32 + 27, lanes]
                            + ACC[RH + t * 32:RH + t * 32 + 27, lanes])

                @pl.loop(0, 2 * TH)
                def _(d):
                    m = lax.rem(g + d, jnp.int32(2 * TH))
                    rs_send(it, lax.div(m, jnp.int32(TH)) * T + part * TH
                            + lax.rem(m, jnp.int32(TH)))

    def point_scatter(it):
        take(EB.at[it], e_r.at[it])

        @pl.loop(0, NG)
        def _(k):
            h = z_at(k)
            cols = pl.ds(pl.multiple_of(h * SLOT, SLOT), SLOT)
            e0, e1 = EB[it, h, :, 0:SLOT], EB[it, h, :, SLOT:2 * SLOT]
            hi, lo = split(jp[0:3, cols] * e0 + jp[3:6, cols] * e1)
            v = jnp.concatenate([hi, lo, jnp.zeros((2, SLOT), F32)], axis=0)
            point_lhs(0, cols, v, APROW[:, cols])

        point_sum(0)
        return PV[0:3, :] + PV[3:6, :]

    mark("ag0")
    gather_all(0, cz)
    XE[0] = crhs
    XE[1] = cmat

    def to_final(src, dst, n):
        return pltpu.make_async_remote_copy(
            src, dst, pe_s.at[n], pe_r.at[n], device_id=final, device_id_type=MESH)

    def final_start(src, dst, n):
        @pl.when(jnp.logical_not(stays))
        def _():
            to_final(src, dst, n).start()

        @pl.when(stays)
        def _():
            pltpu.make_async_copy(src, dst, pe_r.at[n]).start()

    final_start(XE, XEG, 0)
    mark("terms0")
    cam_errors(0)
    mark("scat0")
    cam_scatter(0)
    mark("pscat0")
    pq = point_scatter(0) + damping * PVEC[2]
    pw = pq / PVEC[1]
    PVEC[3] = pq
    PVEC[4] = pw
    mark("pt_gather1")
    point_gather(4, 1)
    G[3:4, :] += fold(pq * pw)
    G[4:5, :] += fold(PVEC[2] * pw)
    G[5:6, :] += fold(pw * pw)

    mark("rs0_wait")
    cq = rs_sum(0, SB[0, mine_k]) + damping * CV[2]
    cw = cq / CV[1]
    CV[3] = cq
    CV[4] = cw
    G[3:4, :] += fold(cq * cw)
    G[4:5, :] += fold(CV[2] * cw)
    G[5:6, :] += fold(cw * cw)
    XQ[...] = cq
    mark("ag1")
    gather_all(1, cw)
    final_start(XQ, XQG, 1)
    mark("terms1")
    cam_errors(1)

    slot = c * NG + g

    def gp_copy(gt, ct):
        return pltpu.make_async_remote_copy(
            GP.at[slot], GP.at[slot], gp_s, gp_r,
            device_id=(gt, 2 * z + ct), device_id_type=MESH)

    mark("scat1")
    cam_scatter(1)
    mark("rs1_wait")
    XV[...] = rs_sum(1, SB[1, mine_k]) + damping * CV[4]
    mark("perm")
    final_start(XV, XG, 2)
    mark("gram_z")

    take(GZ.at[pl.ds(0, NG - 1)], gz_r)
    GZ[z] = GS[...]
    GP[slot] = jnp.sum(GZ[...], axis=0)
    gp_copy(g, 1 - c).start()

    @pl.loop(1, NG)
    def _(d):
        gp_copy(g_at(d), c).start()
        gp_copy(g_at(d), 1 - c).start()

    mark("pscat1")
    PVEC[5] = point_scatter(1) + damping * PVEC[4]

    mark("gram_p")

    take(GP.at[pl.ds(0, 2 * NG - 1)], gp_r)
    mark("final")
    total = jnp.sum(GP[...], axis=0)
    n0, zz, ee, qw, zw, ww, eu, uu = (total[:, i:i + 1] for i in range(8))
    alpha0 = n0 / (damping * zz + ee)
    n1 = alpha0 * alpha0 * qw - n0
    grow = 1.0 + n1 / n0
    curve1 = (grow * grow * (damping * zz + ee) - 2.0 * grow * alpha0 * (damping * zw + eu)
              + alpha0 * alpha0 * (damping * ww + uu))
    alpha1 = n1 / curve1
    xz = alpha0 + alpha1 * grow
    xw = alpha1 * alpha0

    xp[...] = xz * PVEC[2] - xw * PVEC[4]
    rp[...] = PVEC[0] - xz * PVEC[3] + xw * PVEC[5]
    results = [pltpu.make_async_copy(a, b, out_s.at[i]) for i, (a, b) in enumerate((
        (xp, xp_out), (rp, rp_out), (xc, xc_out), (rc, rc_out)))]
    results[0].start()
    results[1].start()

    def put(ref, v):
        for j in range(3):
            ref[0:8, j * 128:(j + 1) * 128] = v[j * 8:j * 8 + 8, :]
            ref[8:9, j * 128:(j + 1) * 128] = v[24 + j:25 + j, :]

    pltpu.make_async_copy(XEG, XEG, pe_r.at[0]).wait()
    pltpu.make_async_copy(XQG, XQG, pe_r.at[1]).wait()
    put(xc, (xz * XEG[0] - xw * XQG[...]) / XEG[1])
    results[2].start()
    base = XEG[0] - xz * XQG[...]

    mark("sends")
    others = pl.ds(0, NG - 1)
    take(S.at[others], a2a_s)
    take(R2.at[c], fwd_s)
    take(SB.at[2, others], rs_s.at[2])
    take(SB.at[3, others], rs_s.at[3])
    for it in range(2):
        take(SB.at[it, others], rs_s.at[it])
        take(VB.at[it, others], ag_s.at[it])
        take(PTS.at[it, others], pt_s.at[it])
        take(XS.at[it], x_s.at[it])
        take(ER.at[it, others], e_s.at[it])
    take(GZ.at[others], gz_s)
    take(GP.at[pl.ds(0, 2 * NG - 1)], gp_s)

    @pl.when(jnp.logical_not(stays))
    def _():
        to_final(XE, XEG, 0).wait_send()
        to_final(XQ, XQG, 1).wait_send()
        to_final(XV, XG, 2).wait_send()

    mark("perm_wait")
    pltpu.make_async_copy(XG, XG, pe_r.at[2]).wait()
    put(rc, base + xw * XG[...])
    results[3].start()
    for m in results:
        m.wait()
    mark(None)


def shards(jac_point, jac_cam, resid, point_index, cam_index):
    NG = lax.axis_size("grp")
    OBS = jac_point.shape[1]
    NPTS = P_DEV
    T = NG // 2
    ROWS = T * 32
    NA = NPTS // 256
    vm = pltpu.VMEM
    dma = pltpu.SemaphoreType.DMA
    QB = min(BLOCKS, NG)
    scratch = [
        vm((6, OBS), F32), vm((18, OBS), F32), vm((2, OBS), F32),
        vm((1, OBS), I32), vm((1, OBS), I32), dma((5,)),
        vm((NG, 21, SLOT), F32), vm((2, NG, 21, SLOT), F32),
        vm((256, 2 * OBS), BF16), vm((256, OBS), BF16),
        vm((256, max(4, 2 * min(6, NG // 2)) * SLOT), BF16),
        vm((4 * ROWS, 4 * SLOT), BF16),
        vm((2 * ROWS // min(2, T), min(4 * SLOT * QB, 2 * OBS)), BF16), vm((2 * NA * 8, OBS), BF16),
        vm((4 * ROWS, 256), F32), vm((1, 2 * OBS), F32), vm((1, OBS), F32),
        vm((2 * ROWS, 256), BF16), vm((NA * 8, 256), BF16),
        vm((2 * ROWS, 2 * min(6, NG // 2) * SLOT), BF16),
        vm((4, NG, 27, 128), F32), vm((4, NG, 27, 128), F32),
        vm((2, NG, 27, 128), F32), vm((5, 27, 128), F32),
        vm((8, NPTS), F32), vm((6, 3, NPTS), F32),
        vm((2, NG, 1, 2 * SLOT), F32), vm((2, NG, 1, 2 * SLOT), F32),
        vm((2, 2 * NG, 1, 2 * SLOT), F32), vm((2, 2 * NG, 1, 2 * SLOT), F32),
        vm((2, 2 * NG, 1, 2 * SLOT), F32), vm((2, NG, 1, 2 * SLOT), F32),
        vm((8, 128), F32), vm((1, 128), F32),
        vm((NG, 1, 128), F32), vm((2 * NG, 1, 128), F32),
        vm((2, 27, 128), F32), vm((2, 27, 128), F32),
        vm((27, 128), F32), vm((27, 128), F32),
        vm((27, 128), F32), vm((27, 128), F32),
        dma, dma, dma((NG,)), dma, dma((NG,)),
        dma((4,)), dma((4,)), dma((2,)), dma((2,)),
        dma((2,)), dma((2, NG // QB)), dma((2,)), dma((2, NG // QB)),
        dma((2,)), dma((2,)), dma, dma, dma, dma,
        dma((3,)), dma((3,)),
    ]
    outs = ((3, NPTS), (9, CAM_DEV), (3, NPTS), (9, CAM_DEV))
    made = pl.pallas_call(
        functools.partial(kernel, NG, OBS, NPTS),
        name="cg",
        out_shape=tuple(jax.ShapeDtypeStruct(s, F32) for s in outs),
        in_specs=[pl.BlockSpec(memory_space=pltpu.HBM)] * 5,
        out_specs=tuple(pl.BlockSpec(memory_space=pltpu.HBM) for _ in outs),
        scratch_shapes=scratch + [vm(s, F32) for s in outs] + [dma((4,))],
        compiler_params=pltpu.CompilerParams(
            collective_id=0, has_side_effects=True, vmem_limit_bytes=VMEM_ALL),
    )(jac_point, jac_cam, resid, point_index.reshape(1, OBS), cam_index.reshape(1, OBS))
    return pl.pallas_call(
        store,
        name="store",
        out_shape=tuple(jax.ShapeDtypeStruct(s, F32) for s in outs),
        in_specs=[pl.BlockSpec(memory_space=pltpu.HBM)] * 4,
        out_specs=tuple(pl.BlockSpec(memory_space=pltpu.HBM) for _ in outs),
        scratch_shapes=[vm(s, F32) for s in outs] + [dma((4,)), dma((4,))],
        compiler_params=pltpu.CompilerParams(vmem_limit_bytes=VMEM_ALL),
    )(*made)


def store(*refs):
    got, sent = refs[12], refs[13]
    loads = [pltpu.make_async_copy(refs[i], refs[8 + i], got.at[i]) for i in range(4)]
    stores = [pltpu.make_async_copy(refs[8 + i], refs[4 + i], sent.at[i]) for i in range(4)]
    for m in loads:
        m.start()
    for i in range(4):
        loads[i].wait()
        stores[i].start()
    for m in stores:
        m.wait()


P_DEV = 4096
VMEM_ALL = 67043328
BLOCKS = 4


def solution(mesh):
    cols, flat = P(None, ("grp", "tile")), P(("grp", "tile"))
    return jax.shard_map(
        shards, mesh=mesh, in_specs=(cols, cols, cols, flat, flat),
        out_specs=(cols,) * 4, check_vma=False)
```
